256 devices in a mesh: tx: 32 (over z, y), ty: 8 (over x, core).
Axes of the slice: x: 4, y: 4, z: 8, core: 2. Of those that a mesh axis runs over, the one named last changes fastest.
Arguments:
- probes: bfloat16 [4096, 1024, 128], P('tx', 'ty')
- filter_taps: float32 [2, 2, 33], replicated, may hold values from 0.05 to 1
- cluster_ranks: int32 [5, 32, 8], replicated, may hold values from 64 to 128
Outputs:
- leaf_basis: bfloat16 [4096, 1024, 128], P('tx', 'ty')
- transfers: float32 [32, 8, 4, 128, 128], P('tx', 'ty')
The draws below stay inside these ranges and needn't reach their ends.
Inputs may be any that keep to these rules, and one draw needn't show every extreme that they name: `cluster_ranks`: only the entry of a cluster's first leaf (lowest row and column indices) is its rank at that level.
All inputs are finite; a program needn't handle non-finite values.
Results may differ from the reference program's by a relative error of at most 0.014.
The reference program's roundings to bfloat16 on the way (of `combined`, `middle`, `sketch` and `weights`) count: a program that leaves them out, or rounds other values in their place, can miss the bound.
Values may be sent and summed in bfloat16 or wider, within the bound.
A program may use at most 128 MiB of HBM per device.

```python
import math
import jax
import jax.numpy as jnp
from jax import lax

TILE = 128
P_SIZE = 128
TAPS = 33
LEVELS = 4
REACH = 80
NX = 4096
NY = 1024
N_TX = 32
N_TY = 8


def draw_probes(key, part):
    first_key, second_key, third_key = jax.random.split(key, 3)
    blocks_x = NX // TILE
    blocks_y = NY // TILE
    half = P_SIZE // 2
    spread = jax.random.uniform(first_key, (blocks_x, blocks_y), jnp.float32, 0.0, math.log(10.0))
    noise = jnp.clip(jax.random.normal(second_key, (NX, NY, P_SIZE), jnp.float32), -6.0, 6.0)
    shared = jnp.clip(jax.random.normal(third_key, (NX, NY), jnp.float32), -6.0, 6.0)
    channel = jnp.arange(P_SIZE).astype(jnp.float32)
    steps_down = -2.0 * channel / max(half - 1, 1)
    own_scale = jnp.where(channel < half, jnp.power(10.0, steps_down), 1.0)
    shared_scale = jnp.where(channel < half, 1.0 / math.sqrt(half), 0.0)
    values = noise * own_scale[None, None, :] + shared[:, :, None] * shared_scale[None, None, :]
    scales = jnp.exp(spread)
    scales = jnp.repeat(jnp.repeat(scales, TILE, axis=0), TILE, axis=1)
    return (values * scales[:, :, None]).astype(jnp.bfloat16)


def place_ends(entries, own_key, smallest, high):
    dims = entries.shape
    place = [jax.random.randint(jax.random.fold_in(own_key, axis), (), 0, dims[axis]) for axis in range(len(dims))]
    entries = entries.at[tuple(place)].set(smallest)
    longest = dims.index(max(dims))
    place[longest] = (place[longest] + 1) % dims[longest]
    return entries.at[tuple(place)].set(high)


def setup_inputs(seed: int = 0) -> dict:
    streams_of = jax.random.split(jax.random.key(seed), 4)
    return {
        "probes": draw_probes(jax.random.fold_in(streams_of[3], 71), 0),
        "filter_taps": jnp.clip(jnp.exp(jax.random.uniform(streams_of[1], (2, 2, TAPS), jnp.float32, math.log(0.05), math.log(1.0))), 0.05, 1.0),
        "cluster_ranks": place_ends(jax.random.randint(streams_of[2], (LEVELS + 1, N_TX, N_TY), P_SIZE // 2, P_SIZE + 1), jax.random.fold_in(streams_of[2], 1), P_SIZE // 2, P_SIZE).astype(jnp.int32),
    }


def solve_triangular(matrix, right, lower):
    return jax.scipy.linalg.solve_triangular(matrix, right, lower=lower)

def composite(filter_taps):
    count = filter_taps.shape[-1]
    wide = 5 * (count - 1) + 1
    first = jnp.arange(count)[:, None, None]
    second = jnp.arange(count)[None, :, None]
    spot = jnp.arange(wide)[None, None, :]
    table = (first + 4 * second == spot).astype(jnp.float32)
    outer = filter_taps[:, 0, :, None] * filter_taps[:, 1, None, :]
    return jnp.einsum('dab,abm->dm', outer, table, precision=lax.Precision.HIGHEST).astype(jnp.bfloat16)

def factor(gram, keep_mask):
    outer = keep_mask[..., :, None] * keep_mask[..., None, :]
    masked = gram * outer
    trace_sum = jnp.sum(jnp.diagonal(masked, axis1=-2, axis2=-1), axis=-1)
    delta = 0.01 * trace_sum / jnp.sum(keep_mask, axis=-1)
    ident = jnp.eye(gram.shape[-1], dtype=jnp.float32)
    shifted = masked + ident * (1.0 - keep_mask)[..., None, :] + delta[..., None, None] * ident * keep_mask[..., None, :]
    return (masked, jnp.linalg.cholesky(shifted))

def products(zeta):
    return jnp.einsum('...kp,...kq->...pq', zeta, zeta, precision=lax.Precision.HIGHEST)

def transfer(lower, keep_mask, child_z):
    right = keep_mask[..., :, None] * jnp.swapaxes(child_z, -1, -2)
    return jnp.swapaxes(solve_triangular(lower, right, lower=True), -1, -2)

def rank_mask(rank_value, width):
    return (jnp.arange(width) < rank_value[..., None]).astype(jnp.float32)

def convolve(probes, combined):
    kernel_x = combined[0].astype(jnp.float32).reshape(1, 1, -1, 1)
    kernel_y = combined[1].astype(jnp.float32).reshape(1, 1, 1, -1)
    groups = probes.reshape(NX, NY, P_SIZE // 8, 8)

    def one_group(index):
        block = lax.dynamic_index_in_dim(groups, index, 2, keepdims=False)
        field = jnp.transpose(block, (2, 0, 1))[:, None].astype(jnp.float32)
        middle = lax.conv_general_dilated(field, kernel_x, (1, 1), ((REACH, REACH), (0, 0)), precision=lax.Precision.HIGHEST)
        middle = lax.optimization_barrier(middle.astype(jnp.bfloat16)).astype(jnp.float32)
        result = lax.conv_general_dilated(middle, kernel_y, (1, 1), ((0, 0), (REACH, REACH)), precision=lax.Precision.HIGHEST)
        return result[:, 0].astype(jnp.bfloat16)
    stacked = lax.map(one_group, jnp.arange(P_SIZE // 8, dtype=jnp.int32))
    return jnp.transpose(stacked.reshape(P_SIZE, NX, NY), (1, 2, 0))

def reference(probes, filter_taps, cluster_ranks):
    combined = composite(filter_taps)
    sketch = convolve(probes, combined)
    tiles = sketch.reshape(N_TX, TILE, N_TY, TILE, P_SIZE)

    def tile_gram(block):
        wide_block = block.astype(jnp.float32)
        return jnp.einsum('ibjp,ibjq->bpq', wide_block, wide_block, precision=lax.Precision.HIGHEST)
    gram = lax.map(tile_gram, tiles) / (TILE * TILE)
    keep_mask = rank_mask(cluster_ranks[0], P_SIZE)
    masked, lower = factor(gram, keep_mask)
    diag_mask = jnp.eye(P_SIZE, dtype=jnp.float32) * keep_mask[..., None, :]
    weights = jnp.swapaxes(solve_triangular(lower, diag_mask, lower=True), -1, -2).astype(jnp.bfloat16)

    def tile_basis(pair):
        block, weight = pair
        return jnp.einsum('ibjp,bpq->ibjq', block.astype(jnp.float32), weight.astype(jnp.float32), precision=lax.Precision.HIGHEST).astype(jnp.bfloat16)
    leaf_basis = lax.map(tile_basis, (tiles, weights)).reshape(NX, NY, P_SIZE)
    zeta = solve_triangular(lower, masked, lower=True)
    grams = products(zeta)
    span_x, span_y = (1, 1)
    results = []
    for level in range(1, 5):
        if level % 2 == 1:
            merged = (grams[0::2] + grams[1::2]) * 0.5
            next_x, next_y, along = (span_x * 2, span_y, 0)
        else:
            merged = (grams[:, 0::2] + grams[:, 1::2]) * 0.5
            next_x, next_y, along = (span_x, span_y * 2, 1)
        keep_mask = rank_mask(cluster_ranks[level, ::next_x, ::next_y], P_SIZE)
        masked, lower = factor(merged, keep_mask)
        lower_child = jnp.repeat(lower, 2, axis=along)
        mask_child = jnp.repeat(keep_mask, 2, axis=along)
        moved = transfer(lower_child, mask_child, zeta)
        results.append(jnp.repeat(jnp.repeat(moved, span_x, axis=0), span_y, axis=1))
        zeta = solve_triangular(lower, masked, lower=True)
        grams = products(zeta)
        span_x, span_y = (next_x, next_y)
    return (leaf_basis, jnp.stack(results, axis=2))
```

```python
import jax
import jax.numpy as jnp
from jax import lax
from jax.experimental import pallas as pl
from jax.experimental.pallas import tpu as pltpu
from jax.sharding import PartitionSpec as P

HIGHEST = lax.Precision.HIGHEST
F = jnp.float32


def extended(block, sides, width):
    for axis, dim in sides:
        count = lax.axis_size(axis)
        forward = [(i, i + 1) for i in range(count - 1)]
        backward = [(target, source) for source, target in forward]
        low = lax.ppermute(
            lax.slice_in_dim(block, block.shape[dim] - width, None, axis=dim), axis, forward
        )
        high = lax.ppermute(lax.slice_in_dim(block, 0, width, axis=dim), axis, backward)
        block = jnp.concatenate([low, block, high], axis=dim)
    return block


def from_partner(shard, axis, stride):
    return lax.ppermute(shard, axis, [(i, i ^ 1 << stride) for i in range(lax.axis_size(axis))])


def composite(filter_taps):
    count = filter_taps.shape[-1]
    wide = 5 * (count - 1) + 1
    first = jnp.arange(count)[:, None, None]
    second = jnp.arange(count)[None, :, None]
    spot = jnp.arange(wide)[None, None, :]
    table = (first + 4 * second == spot).astype(jnp.float32)
    outer = filter_taps[:, 0, :, None] * filter_taps[:, 1, None, :]
    return jnp.einsum("dab,abm->dm", outer, table, precision=lax.Precision.HIGHEST).astype(
        jnp.bfloat16
    )


def toeplitz(line_taps, length):
    wide = line_taps.shape[0]
    columns = length + wide - 1
    pattern = jnp.concatenate([line_taps, jnp.zeros((length,), line_taps.dtype)])
    return jnp.tile(pattern, length)[: length * columns].reshape(length, columns)


def lane_of(x, i): return jnp.broadcast_to(x[:, i:i+1], (8,128))
def row_of(x, i): return jnp.broadcast_to(x[i:i+1,:], (8,128))

def eliminate(X):
    sub=lax.broadcasted_iota(jnp.int32,(8,128),0); lane=lax.broadcasted_iota(jnp.int32,(8,128),1)
    X=list(X); out=[]
    for b in range(16):
        j=8*b
        head=X[b]
        B=[lane_of(head,j+c) for c in range(8)]
        C={t:[lane_of(X[t],j+c) for c in range(8)] for t in range(b+1,16)}
        inblk=(lane>=j)&(lane<j+8)
        head=jnp.where(inblk,jnp.where(lane-j==sub,1.0,0.0),head)
        V=jnp.zeros((8,128),F)
        for c in range(8):
            d=row_of(B[c],c)
            inv=1.0/d
            prow=row_of(head,c)
            V=jnp.where(sub==c,prow*lax.rsqrt(d),V)
            prow=prow*inv
            col=B[c]
            head=jnp.where(sub==c,prow,head-col*prow)
            for e in range(c+1,8):
                brow=row_of(B[e],c)*inv
                B[e]=jnp.where(sub==c,brow,B[e]-col*brow)
        out.append(jnp.where(lane<=j+sub,V,0.0))
        rows=[row_of(head,c) for c in range(8)]
        for t in range(b+1,16):
            acc=jnp.where(inblk,0.0,X[t])
            p=[C[t][c]*rows[c] for c in range(8)]
            s=((p[0]+p[1])+(p[2]+p[3]))+((p[4]+p[5])+(p[6]+p[7]))
            X[t]=acc-s
    return out

def factor(g, rank):
    row=lax.broadcasted_iota(jnp.int32,(128,128),0); col=lax.broadcasted_iota(jnp.int32,(128,128),1)
    keep=(row<rank)&(col<rank)
    masked=jnp.where(keep,g,0.0)
    eye=row==col
    trace=jnp.sum(jnp.where(eye,masked,0.0),keepdims=True)
    delta=0.01*trace/jnp.full((1,1),rank,jnp.int32).astype(F)
    a=masked*(1.0/delta)+jnp.where(eye,1.0,0.0)
    linv=jnp.concatenate(eliminate([a[8*t:8*t+8] for t in range(16)]),axis=0)
    linv=jnp.where(keep,linv*lax.rsqrt(delta),0.0)
    return masked, linv

def dot(a, b):
    return jnp.dot(a, b, precision=HIGHEST, preferred_element_type=F)


def dot_tn(a, b):
    return lax.dot_general(a, b, (((0,), (0,)), ((), ())), precision=HIGHEST, preferred_element_type=F)


def dot_nt(a, b):
    return lax.dot_general(a, b, (((1,), (1,)), ((), ())), precision=HIGHEST, preferred_element_type=F)


def leaf_kernel(rank_ref, gram_ref, weights_ref, zeta_ref, h_ref):
    masked, linv = factor(gram_ref[...], rank_ref[0])
    weights_ref[...] = linv.T.astype(jnp.bfloat16)
    zeta = dot(linv, masked)
    zeta_ref[...] = zeta
    h_ref[...] = dot_tn(zeta, zeta)


def merge_kernel(rank_ref, own_ref, partner_ref, child_ref, moved_ref, zeta_ref, h_ref):
    masked, linv = factor((own_ref[...] + partner_ref[...]) * 0.5, rank_ref[0])
    moved_ref[...] = dot_nt(child_ref[...], linv)
    zeta = dot(linv, masked)
    zeta_ref[...] = zeta
    h_ref[...] = dot_tn(zeta, zeta)


def square(dtype=F):
    return jax.ShapeDtypeStruct((128, 128), dtype)


def specs(count):
    return [pl.BlockSpec(memory_space=pltpu.SMEM)] + [pl.BlockSpec(memory_space=pltpu.VMEM)] * count


def climb_level(child_z, own_gram, partner_gram, rank):
    return pl.pallas_call(
        merge_kernel, out_shape=(square(), square(), square()), in_specs=specs(3)
    )(rank, own_gram, partner_gram, child_z)


def local(probes, filter_taps, cluster_ranks):
    combined = composite(filter_taps)
    reach = (combined.shape[1] - 1) // 2
    rows, cols, width = probes.shape
    tall = extended(probes, (("tx", 0),), reach)
    middle = jnp.dot(
        toeplitz(combined[0], rows),
        tall.reshape(tall.shape[0], cols * width),
        preferred_element_type=jnp.float32,
    )
    middle = middle.reshape(rows, cols, width).astype(jnp.bfloat16)
    broad = extended(middle, (("ty", 1),), reach)
    sketch = jnp.einsum(
        "yc,xcp->xyp", toeplitz(combined[1], cols), broad, preferred_element_type=jnp.float32
    ).astype(jnp.bfloat16)
    flat = sketch.reshape(rows * cols, width)
    gram = jnp.einsum("np,nq->pq", flat, flat, preferred_element_type=jnp.float32) / (rows * cols)
    row_at = lax.axis_index("tx")
    col_at = lax.axis_index("ty")
    rank = cluster_ranks[0, row_at, col_at].reshape(1)
    weights, zeta, grams = pl.pallas_call(
        leaf_kernel, out_shape=(square(jnp.bfloat16), square(), square()), in_specs=specs(1)
    )(rank, gram)
    leaf_basis = (
        jnp.dot(flat, weights, preferred_element_type=jnp.float32)
        .astype(jnp.bfloat16)
        .reshape(rows, cols, width)
    )
    row_two = row_at - row_at % 2
    row_four = row_at - row_at % 4
    col_two = col_at - col_at % 2
    col_four = col_at - col_at % 4
    partner = from_partner(grams, "tx", 0)
    first_e, zeta, grams = climb_level(
        zeta, grams, partner, cluster_ranks[1, row_two, col_at].reshape(1)
    )
    partner = from_partner(grams, "ty", 0)
    second_e, zeta, grams = climb_level(
        zeta, grams, partner, cluster_ranks[2, row_two, col_two].reshape(1)
    )
    partner = from_partner(grams, "tx", 1)
    third_e, zeta, grams = climb_level(
        zeta, grams, partner, cluster_ranks[3, row_four, col_two].reshape(1)
    )
    partner = from_partner(grams, "ty", 1)
    fourth_e, zeta, grams = climb_level(
        zeta, grams, partner, cluster_ranks[4, row_four, col_four].reshape(1)
    )
    transfers = jnp.stack([first_e, second_e, third_e, fourth_e], axis=0)[None, None]
    return (leaf_basis, transfers)


def solution(mesh):
    in_specs = (P("tx", "ty", None), P(), P())
    out_specs = (P("tx", "ty", None), P("tx", "ty", None, None, None))
    return jax.shard_map(local, mesh=mesh, in_specs=in_specs, out_specs=out_specs, check_vma=False)
```

```python
import jax
import jax.numpy as jnp
from jax import lax
from jax.experimental import pallas as pl
from jax.experimental.pallas import tpu as pltpu
from jax.sharding import PartitionSpec as P

HIGHEST = lax.Precision.HIGHEST
F = jnp.float32


def composite(filter_taps):
    count = filter_taps.shape[-1]
    wide = 5 * (count - 1) + 1
    first = jnp.arange(count)[:, None, None]
    second = jnp.arange(count)[None, :, None]
    spot = jnp.arange(wide)[None, None, :]
    table = (first + 4 * second == spot).astype(jnp.float32)
    outer = filter_taps[:, 0, :, None] * filter_taps[:, 1, None, :]
    return jnp.einsum("dab,abm->dm", outer, table, precision=lax.Precision.HIGHEST).astype(
        jnp.bfloat16
    )


def lane_of(x, i): return jnp.broadcast_to(x[:, i:i+1], (8,128))
def row_of(x, i): return jnp.broadcast_to(x[i:i+1,:], (8,128))

def eliminate(X):
    sub=lax.broadcasted_iota(jnp.int32,(8,128),0); lane=lax.broadcasted_iota(jnp.int32,(8,128),1)
    X=list(X); out=[]
    for b in range(16):
        j=8*b
        head=X[b]
        B=[lane_of(head,j+c) for c in range(8)]
        C={t:[lane_of(X[t],j+c) for c in range(8)] for t in range(b+1,16)}
        inblk=(lane>=j)&(lane<j+8)
        head=jnp.where(inblk,jnp.where(lane-j==sub,1.0,0.0),head)
        V=jnp.zeros((8,128),F)
        for c in range(8):
            d=row_of(B[c],c)
            inv=1.0/d
            prow=row_of(head,c)
            V=jnp.where(sub==c,prow*lax.rsqrt(d),V)
            prow=prow*inv
            col=B[c]
            head=jnp.where(sub==c,prow,head-col*prow)
            for e in range(c+1,8):
                brow=row_of(B[e],c)*inv
                B[e]=jnp.where(sub==c,brow,B[e]-col*brow)
        out.append(jnp.where(lane<=j+sub,V,0.0))
        rows=[row_of(head,c) for c in range(8)]
        for t in range(b+1,16):
            acc=jnp.where(inblk,0.0,X[t])
            p=[C[t][c]*rows[c] for c in range(8)]
            s=((p[0]+p[1])+(p[2]+p[3]))+((p[4]+p[5])+(p[6]+p[7]))
            X[t]=acc-s
    return out

def factor(g, rank):
    row=lax.broadcasted_iota(jnp.int32,(128,128),0); col=lax.broadcasted_iota(jnp.int32,(128,128),1)
    keep=(row<rank)&(col<rank)
    masked=jnp.where(keep,g,0.0)
    eye=row==col
    trace=jnp.sum(jnp.where(eye,masked,0.0),keepdims=True)
    delta=0.01*trace/jnp.full((1,1),rank,jnp.int32).astype(F)
    a=masked*(1.0/delta)+jnp.where(eye,1.0,0.0)
    linv=jnp.concatenate(eliminate([a[8*t:8*t+8] for t in range(16)]),axis=0)
    linv=jnp.where(keep,linv*lax.rsqrt(delta),0.0)
    return masked, linv

def dot(a, b):
    return jnp.dot(a, b, precision=HIGHEST, preferred_element_type=F)


def dot_tn(a, b):
    return lax.dot_general(a, b, (((0,), (0,)), ((), ())), precision=HIGHEST, preferred_element_type=F)


def dot_nt(a, b):
    return lax.dot_general(a, b, (((1,), (1,)), ((), ())), precision=HIGHEST, preferred_element_type=F)


MESH = pl.DeviceIdType.MESH


def partner_of(level, row_at, col_at):
    step = (level + 1) // 2
    odd = level % 2
    row = row_at + odd * step * (1 - 2 * ((row_at // step) % 2))
    col = col_at + (1 - odd) * step * (1 - 2 * ((col_at // step) % 2))
    return row, col


def tree_kernel(
    ranks, gram_ref, weights_ref, moved_ref, own, other, zeta_ref, send_sem, recv_sem
):
    row_at, col_at = lax.axis_index("tx"), lax.axis_index("ty")
    barrier = pltpu.get_barrier_semaphore()

    @pl.loop(1, 5)
    def _(level):
        pl.semaphore_signal(
            barrier, inc=1, device_id=partner_of(level, row_at, col_at), device_id_type=MESH
        )

    def swap(level):
        return pltpu.make_async_remote_copy(
            src_ref=own.at[level],
            dst_ref=other.at[level],
            send_sem=send_sem.at[level],
            recv_sem=recv_sem.at[level],
            device_id=partner_of(level, row_at, col_at),
            device_id_type=MESH,
        )

    masked, linv = factor(gram_ref[...], ranks[0, row_at, col_at])
    zeta = dot(linv, masked)
    zeta_ref[...] = zeta
    own[1] = dot_tn(zeta, zeta)
    pl.semaphore_wait(barrier, 4)
    swap(1).start()
    weights_ref[...] = linv.T.astype(jnp.bfloat16)

    @pl.loop(1, 5)
    def _(level):
        span_x = jnp.where(level < 3, 2, 4)
        span_y = jnp.where(level < 2, 1, jnp.where(level < 4, 2, 4))
        rank = ranks[level, row_at - row_at % span_x, col_at - col_at % span_y]
        swap(level).wait_recv()
        masked, linv = factor((own[level] + other[level]) * 0.5, rank)
        child = zeta_ref[...]

        @pl.when(level < 4)
        def _():
            zeta = dot(linv, masked)
            zeta_ref[...] = zeta
            own[level + 1] = dot_tn(zeta, zeta)
            swap(level + 1).start()

        moved_ref[0, 0, level - 1] = dot_nt(child, linv)

    @pl.loop(1, 5)
    def _(level):
        swap(level).wait_send()


def tree(ranks, gram):
    return pl.pallas_call(
        tree_kernel,
        out_shape=(
            jax.ShapeDtypeStruct((128, 128), jnp.bfloat16),
            jax.ShapeDtypeStruct((1, 1, 4, 128, 128), F),
        ),
        in_specs=[
            pl.BlockSpec(memory_space=pltpu.SMEM),
            pl.BlockSpec(memory_space=pltpu.VMEM),
        ],
        out_specs=(
            pl.BlockSpec(memory_space=pltpu.VMEM),
            pl.BlockSpec(memory_space=pltpu.VMEM),
        ),
        scratch_shapes=[
            pltpu.VMEM((5, 128, 128), F),
            pltpu.VMEM((5, 128, 128), F),
            pltpu.VMEM((128, 128), F),
            pltpu.SemaphoreType.DMA((5,)),
            pltpu.SemaphoreType.DMA((5,)),
        ],
        compiler_params=pltpu.CompilerParams(collective_id=1, has_side_effects=True),
        name="tree",
    )(ranks, gram)


def basis_kernel(flat_ref, weights_ref, out_ref):
    out_ref[...] = jnp.dot(
        flat_ref[...], weights_ref[...], preferred_element_type=F
    ).astype(jnp.bfloat16)


def basis(flat, weights):
    rows = 2048
    return pl.pallas_call(
        basis_kernel,
        grid=(flat.shape[0] // rows,),
        out_shape=jax.ShapeDtypeStruct(flat.shape, jnp.bfloat16),
        in_specs=[
            pl.BlockSpec((rows, 128), lambda i: (i, 0)),
            pl.BlockSpec((128, 128), lambda i: (0, 0)),
        ],
        out_specs=pl.BlockSpec((rows, 128), lambda i: (i, 0)),
        name="basis",
    )(flat, weights)


REACH = 80
SIDE = 128
STEPS = 8


def stretched(line, length, width):
    sub = lax.broadcasted_iota(jnp.int32, (8, width), 0)
    base = jnp.broadcast_to(line, (8, width))
    for bit in (1, 2, 4):
        base = jnp.where((sub // bit) % 2 == 1, pltpu.roll(base, bit, 1), base)
    tiles = [base] + [pltpu.roll(base, 8 * t, 1) for t in range(1, length // 8)]
    return jnp.concatenate(tiles, axis=0)


def halo_kernel(
    lines_x, lines_y, probes, sketch, gram_ref, tall, broad, out_slots, mix, across,
    own_sem, out_sem, row_send, row_recv, col_send, col_recv,
):
    n_x, n_y = lax.axis_size("tx"), lax.axis_size("ty")
    row_at, col_at = lax.axis_index("tx"), lax.axis_index("ty")
    has_up, has_down = row_at > 0, row_at < n_x - 1
    has_left, has_right = col_at > 0, col_at < n_y - 1
    up, down = (row_at - 1, col_at), (row_at + 1, col_at)
    left, right = (row_at, col_at - 1), (row_at, col_at + 1)
    sides = ((has_up, up), (has_down, down), (has_left, left), (has_right, right))

    load = pltpu.make_async_copy(probes, tall.at[pl.ds(REACH, SIDE)], own_sem)
    load.start()
    barrier = pltpu.get_barrier_semaphore()
    for there, device in sides:
        @pl.when(there)
        def _():
            pl.semaphore_signal(barrier, inc=1, device_id=device, device_id_type=MESH)
    peers = [there.astype(jnp.int32) for there, _ in sides]
    pl.semaphore_wait(barrier, peers[0] + peers[1] + peers[2] + peers[3])

    def row_copy(to_down, step, first):
        count = 24 if first else 8
        far = 8 * step + 24
        if to_down:
            source, target, device, way = SIDE - far, REACH - far, down, 0
        else:
            source, target, device, way = far - count, REACH + SIDE + far - count, up, 1
        return pltpu.make_async_remote_copy(
            src_ref=probes.at[pl.ds(source, count)],
            dst_ref=tall.at[pl.ds(target, count)],
            send_sem=row_send.at[way, step],
            recv_sem=row_recv.at[way, step],
            device_id=device,
            device_id_type=MESH,
        )

    def col_copy(to_right, step, low):
        rows = 8 * (7 - step) if low else 8 * (8 + step)
        if to_right:
            source, target, device, way = SIDE, 0, right, 0
        else:
            source, target, device, way = REACH, REACH + SIDE, left, 1
        half = 0 if low else 1
        return pltpu.make_async_remote_copy(
            src_ref=broad.at[pl.ds(rows, 8), pl.ds(source, REACH)],
            dst_ref=broad.at[pl.ds(rows, 8), pl.ds(target, REACH)],
            send_sem=col_send.at[way, half, step],
            recv_sem=col_recv.at[way, half, step],
            device_id=device,
            device_id_type=MESH,
        )

    def each(action, step, first=False):
        for there, to_down in ((has_down, True), (has_up, False)):
            @pl.when(there)
            def _():
                action(row_copy(to_down, step, first))

    def each_arrival(step, first=False):
        for there, to_down in ((has_up, True), (has_down, False)):
            @pl.when(there)
            def _():
                row_copy(to_down, step, first).wait_recv()

    start = lambda copy: copy.start()
    sent = lambda copy: copy.wait_send()
    each(start, 0, True)
    each(start, 1)
    mix[...] = stretched(lines_x[...], 128, mix.shape[1]).astype(jnp.bfloat16)
    across[...] = stretched(lines_y[...], 128, across.shape[1]).astype(jnp.bfloat16)

    @pl.when(jnp.logical_not(has_up))
    def _():
        tall[pl.ds(0, REACH)] = jnp.zeros((REACH, SIDE, SIDE), jnp.bfloat16)

    @pl.when(jnp.logical_not(has_down))
    def _():
        tall[pl.ds(REACH + SIDE, REACH)] = jnp.zeros((REACH, SIDE, SIDE), jnp.bfloat16)

    @pl.when(jnp.logical_not(has_left))
    def _():
        broad[:, pl.ds(0, REACH)] = jnp.zeros((SIDE, REACH, SIDE), jnp.bfloat16)

    @pl.when(jnp.logical_not(has_right))
    def _():
        broad[:, pl.ds(REACH + SIDE, REACH)] = jnp.zeros((SIDE, REACH, SIDE), jnp.bfloat16)

    gram_ref[...] = jnp.zeros_like(gram_ref)
    load.wait()

    def filter_rows(step):
        @pl.loop(0, 8)
        def _(index):
            block = index // 4
            rows = pl.multiple_of(8 * (7 - step + block * (1 + 2 * step)), 8)
            cols = pl.multiple_of(32 * (index % 4), 32)
            depth = 8 + 2 * REACH
            pair = [
                tall[pl.ds(rows, depth), pl.ds(cols + 16 * k, 16)].reshape(depth * 16, SIDE)
                for k in range(2)
            ]
            middle = jnp.dot(
                mix[...], jnp.concatenate(pair, axis=1), preferred_element_type=F
            ).astype(jnp.bfloat16)
            for k in range(2):
                broad[pl.ds(rows, 8), pl.ds(REACH + cols + 16 * k, 16)] = middle[
                    :, SIDE * k : SIDE * (k + 1)
                ].reshape(8, 16, SIDE)

    def out_copy(step, half):
        rows = 8 * (7 - step) if half == 0 else 8 * (8 + step)
        return pltpu.make_async_copy(
            out_slots.at[step, pl.ds(8 * half, 8)], sketch.at[pl.ds(rows, 8)], out_sem.at[step, half]
        )

    def send_cols(step):
        for there, to_right in ((has_right, True), (has_left, False)):
            for low in (True, False):
                @pl.when(there)
                def _():
                    col_copy(to_right, step, low).start()

    def filter_cols(step):
        for there, to_right in ((has_left, True), (has_right, False)):
            for low in (True, False):
                @pl.when(there)
                def _():
                    col_copy(to_right, step, low).wait_recv()

        @pl.loop(0, 8)
        def _(index):
            block = index // 4
            rows = 8 * (7 - step + block * (1 + 2 * step)) + 2 * (index % 4)
            pair = [broad[rows + k] for k in range(2)]
            result = jnp.dot(
                across[:, : SIDE + 2 * REACH],
                jnp.concatenate(pair, axis=1),
                preferred_element_type=F,
            ).astype(jnp.bfloat16)
            slot = 2 * index
            for k in range(2):
                out_slots[step, slot + k] = result[:, SIDE * k : SIDE * (k + 1)]

        flat = out_slots[step].reshape(16 * SIDE, SIDE)
        gram_ref[...] += lax.dot_general(
            flat, flat, (((0,), (0,)), ((), ())), preferred_element_type=F
        )
        for half in range(2):
            out_copy(step, half).start()

    each_arrival(0, True)
    filter_rows(0)
    send_cols(0)
    each(sent, 0, True)
    each(start, 2)

    @pl.loop(1, STEPS)
    def _(step):
        each_arrival(step)
        filter_rows(step)
        send_cols(step)
        each(sent, step)

        @pl.when(step < STEPS - 2)
        def _():
            each(start, step + 2)
        filter_cols(step - 1)

    filter_cols(STEPS - 1)

    @pl.loop(0, STEPS)
    def _(step):
        for half in range(2):
            out_copy(step, half).wait()
        for there, to_right in ((has_right, True), (has_left, False)):
            for low in (True, False):
                @pl.when(there)
                def _():
                    col_copy(to_right, step, low).wait_send()

    gram_ref[...] = gram_ref[...] * (1.0 / (SIDE * SIDE))


def halo(lines_x, lines_y, probes):
    bf = jnp.bfloat16
    return pl.pallas_call(
        halo_kernel,
        out_shape=(
            jax.ShapeDtypeStruct((SIDE, SIDE, SIDE), bf),
            jax.ShapeDtypeStruct((SIDE, SIDE), F),
        ),
        in_specs=[
            pl.BlockSpec(memory_space=pltpu.VMEM),
            pl.BlockSpec(memory_space=pltpu.VMEM),
            pl.BlockSpec(memory_space=pl.ANY),
        ],
        out_specs=(
            pl.BlockSpec(memory_space=pl.ANY),
            pl.BlockSpec(memory_space=pltpu.VMEM),
        ),
        scratch_shapes=[
            pltpu.VMEM((SIDE + 2 * REACH, SIDE, SIDE), bf),
            pltpu.VMEM((SIDE, SIDE + 2 * REACH, SIDE), bf),
            pltpu.VMEM((STEPS, 16, SIDE, SIDE), bf),
            pltpu.VMEM((SIDE, 16 * (8 + 2 * REACH)), bf),
            pltpu.VMEM((SIDE, 384), bf),
            pltpu.SemaphoreType.DMA,
            pltpu.SemaphoreType.DMA((STEPS, 2)),
            pltpu.SemaphoreType.DMA((2, STEPS)),
            pltpu.SemaphoreType.DMA((2, STEPS)),
            pltpu.SemaphoreType.DMA((2, 2, STEPS)),
            pltpu.SemaphoreType.DMA((2, 2, STEPS)),
        ],
        compiler_params=pltpu.CompilerParams(
            collective_id=0, has_side_effects=True, vmem_limit_bytes=50 * 2**20
        ),
        name="halo",
    )(lines_x, lines_y, probes)


def local(probes, filter_taps, cluster_ranks):
    combined = composite(filter_taps).astype(F)
    wide = combined.shape[1]
    lines_x = jnp.pad(combined[0][:, None], ((0, 168 - wide), (0, 15))).reshape(1, 168 * 16)
    lines_y = jnp.pad(combined[1][None], ((0, 0), (0, 384 - wide)))
    sketch, gram = halo(lines_x, lines_y, probes)
    weights, transfers = tree(cluster_ranks, gram)
    leaf_basis = basis(sketch.reshape(SIDE * SIDE, SIDE), weights).reshape(probes.shape)
    return (leaf_basis, transfers)


def solution(mesh):
    in_specs = (P("tx", "ty", None), P(), P())
    out_specs = (P("tx", "ty", None), P("tx", "ty", None, None, None))
    return jax.shard_map(local, mesh=mesh, in_specs=in_specs, out_specs=out_specs, check_vma=False)
```

```python
import jax
import jax.numpy as jnp
from jax import lax
from jax.experimental import pallas as pl
from jax.experimental.pallas import tpu as pltpu
from jax.sharding import PartitionSpec as P

HIGHEST = lax.Precision.HIGHEST
F = jnp.float32
BF = jnp.bfloat16
REACH = 80
SIDE = 128
STEPS = 8
MESH = pl.DeviceIdType.MESH


def lane_of(x, i):
    return jnp.broadcast_to(x[:, i : i + 1], (8, 128))


def row_of(x, i):
    return jnp.broadcast_to(x[i : i + 1, :], (8, 128))


def split(a):
    one = a.astype(BF)
    rest = a - one.astype(F)
    two = rest.astype(BF)
    return one, two, (rest - two.astype(F)).astype(BF)


def eliminate(tiles):
    sub = lax.broadcasted_iota(jnp.int32, (8, 128), 0)
    lane = lax.broadcasted_iota(jnp.int32, (8, 128), 1)
    tiles, out = list(tiles), []
    for b in range(8):
        j = 16 * b
        rows = [tiles[2 * b], tiles[2 * b + 1]]
        cols = [[lane_of(rows[h], j + c) for c in range(16)] for h in range(2)]
        near = range(2 * b + 2, min(2 * b + 4, 16))
        below = {t: [lane_of(tiles[t], j + c) for c in range(16)] for t in near}
        a1, a2, a3 = split(jnp.concatenate(rows, axis=0))
        inside = (lane >= j) & (lane < j + 16)
        rows = [
            jnp.where(inside, jnp.where(lane - j == sub + 8 * h, 1.0, 0.0), rows[h]) for h in range(2)
        ]
        kept = [jnp.zeros((8, 128), F) for _ in range(2)]
        for c in range(16):
            h, s = divmod(c, 8)
            pivot = row_of(cols[h][c], s)
            inv = 1.0 / pivot
            line = row_of(rows[h], s)
            kept[h] = jnp.where(sub == s, line * lax.rsqrt(pivot), kept[h])
            line = line * inv
            for g in range(2):
                new = rows[g] - cols[g][c] * line
                rows[g] = jnp.where(sub == s, line, new) if g == h else new
            for e in range(c + 1, 16):
                line_e = row_of(cols[h][e], s) * inv
                for g in range(2):
                    new = cols[g][e] - cols[g][c] * line_e
                    cols[g][e] = jnp.where(sub == s, line_e, new) if g == h else new
        out += [jnp.where(lane <= j + 8 * h + sub, kept[h], 0.0) for h in range(2)]
        lines = [row_of(rows[c // 8], c % 8) for c in range(16)]
        for t in near:
            terms = [below[t][c] * lines[c] for c in range(16)]
            while len(terms) > 1:
                terms = [terms[i] + terms[i + 1] for i in range(0, len(terms), 2)]
            tiles[t] = jnp.where(inside, 0.0, tiles[t]) - terms[0]
        if b < 6:
            b1, b2, b3 = split(jnp.concatenate(rows, axis=0))
            change = lax.dot_general(
                jnp.concatenate([a1, a1, a2, a2, a1, a3], axis=0),
                jnp.concatenate([b1, b2, b1, b2, b3, b1], axis=0),
                (((0,), (0,)), ((), ())),
                preferred_element_type=F,
            )
            for t in range(2 * b + 4, 16):
                tiles[t] = jnp.where(inside, 0.0, tiles[t]) - change[8 * t : 8 * t + 8]
    return out


def factor(g, rank):
    row=lax.broadcasted_iota(jnp.int32,(128,128),0); col=lax.broadcasted_iota(jnp.int32,(128,128),1)
    keep=(row.astype(F)<rank)&(col.astype(F)<rank)
    masked=jnp.where(keep,g,0.0)
    eye=row==col
    trace=jnp.sum(jnp.where(eye,masked,0.0),keepdims=True)
    delta=0.01*trace/rank
    a=masked*(1.0/delta)+jnp.where(eye,1.0,0.0)
    linv=jnp.concatenate(eliminate([a[8*t:8*t+8] for t in range(16)]),axis=0)
    linv=jnp.where(keep,linv*lax.rsqrt(delta),0.0)
    return masked, linv

def dot(a, b):
    return jnp.dot(a, b, precision=HIGHEST, preferred_element_type=F)


def dot_tn(a, b):
    return lax.dot_general(a, b, (((0,), (0,)), ((), ())), precision=HIGHEST, preferred_element_type=F)


def dot_nt(a, b):
    return lax.dot_general(a, b, (((1,), (1,)), ((), ())), precision=HIGHEST, preferred_element_type=F)


def partner_of(level, row_at, col_at):
    step = (level + 1) // 2
    odd = level % 2
    row = row_at + odd * step * (1 - 2 * ((row_at // step) % 2))
    col = col_at + (1 - odd) * step * (1 - 2 * ((col_at // step) % 2))
    return row, col


def combine(taps, pads):
    pads[...] = jnp.zeros_like(pads)
    for which in range(2):
        for dim in range(2):
            pads[which, dim : dim + 1, 0 : taps.shape[2]] = taps[dim, which : which + 1, :]
    first, second = pads[0], pads[1]
    total = jnp.zeros_like(first)
    for b in range(taps.shape[2]):
        moved = pltpu.roll(first, 4 * b, 1) if b else first
        total = total + moved * jnp.broadcast_to(second[:, b : b + 1], first.shape)
    return total.astype(BF)

def stretched(line, length, width):
    sub = lax.broadcasted_iota(jnp.int32, (8, width), 0)
    base = jnp.broadcast_to(line, (8, width))
    for bit in (1, 2, 4):
        base = jnp.where((sub // bit) % 2 == 1, pltpu.roll(base, bit, 1), base)
    tiles = [base] + [pltpu.roll(base, 8 * t, 1) for t in range(1, length // 8)]
    return jnp.concatenate(tiles, axis=0)


def body(
    taps, ranks, probes, sketch, weights_ref, moved_ref,
    tall, broad, out_slots, mix, across, part, gram_ref, taps_ref, ranks_ref, pads, own, other, zeta_ref,
    small_sem, own_sem, out_sem, row_send, row_recv, col_send, col_recv, swap_send, swap_recv,
):
    n_x, n_y = lax.axis_size("tx"), lax.axis_size("ty")
    row_at, col_at = lax.axis_index("tx"), lax.axis_index("ty")
    has_up, has_down = row_at > 0, row_at < n_x - 1
    has_left, has_right = col_at > 0, col_at < n_y - 1
    up, down = (row_at - 1, col_at), (row_at + 1, col_at)
    left, right = (row_at, col_at - 1), (row_at, col_at + 1)
    sides = ((has_up, up), (has_down, down), (has_left, left), (has_right, right))

    load = pltpu.make_async_copy(probes, tall.at[pl.ds(REACH, SIDE)], own_sem)
    load.start()
    small = [
        pltpu.make_async_copy(taps, taps_ref, small_sem.at[0]),
        pltpu.make_async_copy(ranks, ranks_ref, small_sem.at[1]),
    ]
    for copy in small:
        copy.start()
    barrier = pltpu.get_barrier_semaphore()
    for there, device in sides:
        @pl.when(there)
        def _():
            pl.semaphore_signal(barrier, inc=1, device_id=device, device_id_type=MESH)

    @pl.loop(1, 5)
    def _(level):
        pl.semaphore_signal(
            barrier, inc=1, device_id=partner_of(level, row_at, col_at), device_id_type=MESH
        )

    peers = [there.astype(jnp.int32) for there, _ in sides]
    pl.semaphore_wait(barrier, peers[0] + peers[1] + peers[2] + peers[3] + 4)

    def row_copy(to_down, step, first):
        count = 24 if first else 8
        far = 8 * step + 24
        if to_down:
            source, target, device, way = SIDE - far, REACH - far, down, 0
        else:
            source, target, device, way = far - count, REACH + SIDE + far - count, up, 1
        return pltpu.make_async_remote_copy(
            src_ref=probes.at[pl.ds(source, count)],
            dst_ref=tall.at[pl.ds(target, count)],
            send_sem=row_send.at[way, step],
            recv_sem=row_recv.at[way, step],
            device_id=device,
            device_id_type=MESH,
        )

    def col_copy(to_right, step, low):
        rows = 8 * (7 - step) if low else 8 * (8 + step)
        if to_right:
            source, target, device, way = SIDE, 0, right, 0
        else:
            source, target, device, way = REACH, REACH + SIDE, left, 1
        half = 0 if low else 1
        return pltpu.make_async_remote_copy(
            src_ref=broad.at[pl.ds(rows, 8), pl.ds(source, REACH)],
            dst_ref=broad.at[pl.ds(rows, 8), pl.ds(target, REACH)],
            send_sem=col_send.at[way, half, step],
            recv_sem=col_recv.at[way, half, step],
            device_id=device,
            device_id_type=MESH,
        )

    def each(action, step, first=False):
        for there, to_down in ((has_down, True), (has_up, False)):
            @pl.when(there)
            def _():
                action(row_copy(to_down, step, first))

    def each_arrival(step, first=False):
        for there, to_down in ((has_up, True), (has_down, False)):
            @pl.when(there)
            def _():
                row_copy(to_down, step, first).wait_recv()

    start = lambda copy: copy.start()
    sent = lambda copy: copy.wait_send()
    each(start, 0, True)
    each(start, 1)
    for copy in small:
        copy.wait()
    lines = combine(taps_ref, pads)
    wide = mix.shape[1]
    spot = lax.broadcasted_iota(jnp.int32, (256, wide), 1)
    spread = jnp.where(spot == 16 * lax.broadcasted_iota(jnp.int32, (256, wide), 0), 1.0, 0.0)
    line_x = jnp.dot(lines, spread.astype(BF), preferred_element_type=F)[0:1]
    line_y = jnp.concatenate([lines[1:2].astype(F), jnp.zeros((1, 128), F)], axis=1)
    mix[...] = stretched(line_x, 128, wide).astype(BF)
    across[...] = stretched(line_y, 128, across.shape[1]).astype(BF)

    @pl.when(jnp.logical_not(has_up))
    def _():
        tall[pl.ds(0, REACH)] = jnp.zeros((REACH, SIDE, SIDE), BF)

    @pl.when(jnp.logical_not(has_down))
    def _():
        tall[pl.ds(REACH + SIDE, REACH)] = jnp.zeros((REACH, SIDE, SIDE), BF)

    @pl.when(jnp.logical_not(has_left))
    def _():
        broad[:, pl.ds(0, REACH)] = jnp.zeros((SIDE, REACH, SIDE), BF)

    @pl.when(jnp.logical_not(has_right))
    def _():
        broad[:, pl.ds(REACH + SIDE, REACH)] = jnp.zeros((SIDE, REACH, SIDE), BF)

    gram_ref[...] = jnp.zeros_like(gram_ref)
    load.wait()

    def place(step, index):
        block = index // 4
        rows = pl.multiple_of(8 * (7 - step + block * (1 + 2 * step)), 8)
        return block, rows, pl.multiple_of(32 * (index % 4), 32)

    def columns(rows, depth, cols):
        return jnp.concatenate(
            [
                tall[pl.ds(rows, depth), pl.ds(cols + 16 * k, 16)].reshape(depth * 16, SIDE)
                for k in range(2)
            ],
            axis=1,
        )

    def begin_rows(step):
        @pl.loop(0, 8)
        def _(index):
            block, rows, cols = place(step, index)
            near = 8 * (1 - block)
            weight = mix[:, pl.ds(pl.multiple_of(16 * near, 128), 32 * REACH)]
            part[index] = jnp.dot(
                weight, columns(rows + near, 2 * REACH, cols), preferred_element_type=F
            )

    def finish_rows(step):
        @pl.loop(0, 8)
        def _(index):
            block, rows, cols = place(step, index)
            far = 2 * REACH * block
            weight = mix[:, pl.ds(pl.multiple_of(16 * far, 128), 128)]
            middle = (
                part[index]
                + jnp.dot(weight, columns(rows + far, 8, cols), preferred_element_type=F)
            ).astype(BF)
            for k in range(2):
                broad[pl.ds(rows, 8), pl.ds(REACH + cols + 16 * k, 16)] = middle[
                    :, SIDE * k : SIDE * (k + 1)
                ].reshape(8, 16, SIDE)

    def out_copy(step, half):
        rows = 8 * (7 - step) if half == 0 else 8 * (8 + step)
        return pltpu.make_async_copy(
            out_slots.at[step, pl.ds(8 * half, 8)], sketch.at[pl.ds(rows, 8)], out_sem.at[step, half]
        )

    def send_cols(step):
        for there, to_right in ((has_right, True), (has_left, False)):
            for low in (True, False):
                @pl.when(there)
                def _():
                    col_copy(to_right, step, low).start()

    def filter_cols(step):
        for there, to_right in ((has_left, True), (has_right, False)):
            for low in (True, False):
                @pl.when(there)
                def _():
                    col_copy(to_right, step, low).wait_recv()

        @pl.loop(0, 8)
        def _(index):
            block = index // 4
            rows = 8 * (7 - step + block * (1 + 2 * step)) + 2 * (index % 4)
            pair = [broad[rows + k] for k in range(2)]
            result = jnp.dot(
                across[:, : SIDE + 2 * REACH],
                jnp.concatenate(pair, axis=1),
                preferred_element_type=F,
            ).astype(BF)
            slot = 2 * index
            for k in range(2):
                out_slots[step, slot + k] = result[:, SIDE * k : SIDE * (k + 1)]

        flat = out_slots[step].reshape(16 * SIDE, SIDE)
        gram_ref[...] += lax.dot_general(
            flat, flat, (((0,), (0,)), ((), ())), preferred_element_type=F
        )
        for half in range(2):
            out_copy(step, half).start()

    each_arrival(0, True)
    begin_rows(0)

    @pl.loop(0, STEPS)
    def _(step):
        @pl.when(step > 0)
        def _():
            each_arrival(step)
        finish_rows(step)
        send_cols(step)

        @pl.when(step == 0)
        def _():
            each(sent, 0, True)

        @pl.when(step > 0)
        def _():
            each(sent, step)

        @pl.when(step < STEPS - 2)
        def _():
            each(start, step + 2)

        @pl.when(step < STEPS - 1)
        def _():
            begin_rows(step + 1)

        @pl.when(step > 0)
        def _():
            filter_cols(step - 1)

    filter_cols(STEPS - 1)

    def swap(level):
        return pltpu.make_async_remote_copy(
            src_ref=own.at[level],
            dst_ref=other.at[level],
            send_sem=swap_send.at[level],
            recv_sem=swap_recv.at[level],
            device_id=partner_of(level, row_at, col_at),
            device_id_type=MESH,
        )

    def rank_at(level, row, col):
        table = ranks_ref[level]
        spot = (lax.broadcasted_iota(jnp.int32, table.shape, 0) == col) & (
            lax.broadcasted_iota(jnp.int32, table.shape, 1) == row
        )
        return jnp.sum(jnp.where(spot, table, 0).astype(F), keepdims=True)

    masked, linv = factor(gram_ref[...] * (1.0 / (SIDE * SIDE)), rank_at(0, row_at, col_at))
    zeta = dot(linv, masked)
    zeta_ref[...] = zeta
    own[1] = dot_tn(zeta, zeta)
    swap(1).start()
    weights_ref[...] = linv.T.astype(BF)

    @pl.loop(1, 5)
    def _(level):
        span_x = jnp.where(level < 3, 2, 4)
        span_y = jnp.where(level < 2, 1, jnp.where(level < 4, 2, 4))
        rank = rank_at(level, row_at - row_at % span_x, col_at - col_at % span_y)
        swap(level).wait_recv()
        masked, linv = factor((own[level] + other[level]) * 0.5, rank)
        child = zeta_ref[...]

        @pl.when(level < 4)
        def _():
            zeta = dot(linv, masked)
            zeta_ref[...] = zeta
            own[level + 1] = dot_tn(zeta, zeta)
            swap(level + 1).start()

        moved_ref[0, 0, level - 1] = dot_nt(child, linv)

    @pl.loop(1, 5)
    def _(level):
        swap(level).wait_send()

    @pl.loop(0, STEPS)
    def _(step):
        for half in range(2):
            out_copy(step, half).wait()
        for there, to_right in ((has_right, True), (has_left, False)):
            for low in (True, False):
                @pl.when(there)
                def _():
                    col_copy(to_right, step, low).wait_send()


def compress(taps, ranks, probes):
    depth = 8 + 2 * REACH
    return pl.pallas_call(
        body,
        out_shape=(
            jax.ShapeDtypeStruct((SIDE, SIDE, SIDE), BF),
            jax.ShapeDtypeStruct((SIDE, SIDE), BF),
            jax.ShapeDtypeStruct((1, 1, 4, SIDE, SIDE), F),
        ),
        in_specs=[pl.BlockSpec(memory_space=pl.ANY)] * 3,
        out_specs=(
            pl.BlockSpec(memory_space=pl.ANY),
            pl.BlockSpec(memory_space=pltpu.VMEM),
            pl.BlockSpec(memory_space=pltpu.VMEM),
        ),
        scratch_shapes=[
            pltpu.VMEM((SIDE + 2 * REACH, SIDE, SIDE), BF),
            pltpu.VMEM((SIDE, SIDE + 2 * REACH, SIDE), BF),
            pltpu.VMEM((STEPS, 16, SIDE, SIDE), BF),
            pltpu.VMEM((SIDE, 16 * depth), BF),
            pltpu.VMEM((SIDE, 384), BF),
            pltpu.VMEM((8, SIDE, 2 * SIDE), F),
            pltpu.VMEM((SIDE, SIDE), F),
            pltpu.VMEM(taps.shape, F),
            pltpu.VMEM(ranks.shape, jnp.int32),
            pltpu.VMEM((2, 16, 256), F),
            pltpu.VMEM((5, SIDE, SIDE), F),
            pltpu.VMEM((5, SIDE, SIDE), F),
            pltpu.VMEM((SIDE, SIDE), F),
            pltpu.SemaphoreType.DMA((2,)),
            pltpu.SemaphoreType.DMA,
            pltpu.SemaphoreType.DMA((STEPS, 2)),
            pltpu.SemaphoreType.DMA((2, STEPS)),
            pltpu.SemaphoreType.DMA((2, STEPS)),
            pltpu.SemaphoreType.DMA((2, 2, STEPS)),
            pltpu.SemaphoreType.DMA((2, 2, STEPS)),
            pltpu.SemaphoreType.DMA((5,)),
            pltpu.SemaphoreType.DMA((5,)),
        ],
        compiler_params=pltpu.CompilerParams(
            collective_id=0, has_side_effects=True, vmem_limit_bytes=50 * 2**20
        ),
        name="compress",
    )(taps, ranks, probes)


CHUNKS = 8


def basis_kernel(sketch, weights_ref, moved, out, moved_out, source, result, load_sem, store_sem, pass_sem):
    rows = SIDE // CHUNKS

    def part(ref, index):
        return ref.at[pl.ds(rows * index, rows)]

    def load(index):
        return pltpu.make_async_copy(part(sketch, index), part(source, index), load_sem.at[index])

    def store(index):
        return pltpu.make_async_copy(part(result, index), part(out, index), store_sem.at[index])

    for index in range(CHUNKS):
        load(index).start()
    forward = pltpu.make_async_copy(moved, moved_out, pass_sem)
    forward.start()
    weights = weights_ref[...]
    zero = jnp.zeros_like(weights)
    twice = jnp.concatenate(
        [jnp.concatenate([weights, zero], axis=1), jnp.concatenate([zero, weights], axis=1)], axis=0
    )

    @pl.loop(0, CHUNKS)
    def _(index):
        load(index).wait()
        half = rows // 2
        base = rows * index
        pair = [
            source[pl.ds(base + half * k, half)].reshape(half * SIDE, SIDE) for k in range(2)
        ]
        both = jnp.dot(jnp.concatenate(pair, axis=1), twice, preferred_element_type=F).astype(BF)
        for k in range(2):
            result[pl.ds(base + half * k, half)] = both[:, SIDE * k : SIDE * (k + 1)].reshape(
                half, SIDE, SIDE
            )
        store(index).start()

    for index in range(CHUNKS):
        store(index).wait()
    forward.wait()


def basis(sketch, weights, moved):
    anywhere = pl.BlockSpec(memory_space=pl.ANY)
    return pl.pallas_call(
        basis_kernel,
        out_shape=(
            jax.ShapeDtypeStruct(sketch.shape, BF),
            jax.ShapeDtypeStruct(moved.shape, F),
        ),
        in_specs=[anywhere, pl.BlockSpec(memory_space=pltpu.VMEM), anywhere],
        out_specs=(anywhere, anywhere),
        scratch_shapes=[
            pltpu.VMEM(sketch.shape, BF),
            pltpu.VMEM(sketch.shape, BF),
            pltpu.SemaphoreType.DMA((CHUNKS,)),
            pltpu.SemaphoreType.DMA((CHUNKS,)),
            pltpu.SemaphoreType.DMA,
        ],
        compiler_params=pltpu.CompilerParams(vmem_limit_bytes=24 * 2**20),
        name="basis",
    )(sketch, weights, moved)


def local(probes, filter_taps, cluster_ranks):
    sketch, weights, moved = compress(filter_taps, jnp.swapaxes(cluster_ranks, 1, 2), probes)
    return basis(sketch, weights, moved)


def solution(mesh):
    in_specs = (P("tx", "ty", None), P(), P())
    out_specs = (P("tx", "ty", None), P("tx", "ty", None, None, None))
    return jax.shard_map(local, mesh=mesh, in_specs=in_specs, out_specs=out_specs, check_vma=False)
```

```python
import jax
import jax.numpy as jnp
from jax import lax
from jax.experimental import pallas as pl
from jax.experimental.pallas import tpu as pltpu
from jax.sharding import PartitionSpec as P

HIGHEST = lax.Precision.HIGHEST
F = jnp.float32
BF = jnp.bfloat16
REACH = 80
SIDE = 128
STEPS = 8
MESH = pl.DeviceIdType.MESH


def lane_of(x, i):
    return jnp.broadcast_to(x[:, i : i + 1], (8, 128))


def row_of(x, i):
    return jnp.broadcast_to(x[i : i + 1, :], (8, 128))


def split(a):
    one = a.astype(BF)
    rest = a - one.astype(F)
    two = rest.astype(BF)
    return one, two, (rest - two.astype(F)).astype(BF)


def eliminate(tiles):
    sub = lax.broadcasted_iota(jnp.int32, (8, 128), 0)
    lane = lax.broadcasted_iota(jnp.int32, (8, 128), 1)
    tiles, out = list(tiles), []
    for b in range(8):
        j = 16 * b
        rows = [tiles[2 * b], tiles[2 * b + 1]]
        cols = [[lane_of(rows[h], j + c) for c in range(16)] for h in range(2)]
        near = range(2 * b + 2, min(2 * b + 4, 16))
        below = {t: [lane_of(tiles[t], j + c) for c in range(16)] for t in near}
        a1, a2, a3 = split(jnp.concatenate(rows, axis=0))
        inside = (lane >= j) & (lane < j + 16)
        rows = [
            jnp.where(inside, jnp.where(lane - j == sub + 8 * h, 1.0, 0.0), rows[h]) for h in range(2)
        ]
        kept = [jnp.zeros((8, 128), F) for _ in range(2)]
        for c in range(16):
            h, s = divmod(c, 8)
            pivot = row_of(cols[h][c], s)
            inv = 1.0 / pivot
            line = row_of(rows[h], s)
            kept[h] = jnp.where(sub == s, line * lax.rsqrt(pivot), kept[h])
            line = line * inv
            for g in range(2):
                new = rows[g] - cols[g][c] * line
                rows[g] = jnp.where(sub == s, line, new) if g == h else new
            for e in range(c + 1, 16):
                line_e = row_of(cols[h][e], s) * inv
                for g in range(2):
                    new = cols[g][e] - cols[g][c] * line_e
                    cols[g][e] = jnp.where(sub == s, line_e, new) if g == h else new
        out += [jnp.where(lane <= j + 8 * h + sub, kept[h], 0.0) for h in range(2)]
        lines = [row_of(rows[c // 8], c % 8) for c in range(16)]
        for t in near:
            terms = [below[t][c] * lines[c] for c in range(16)]
            while len(terms) > 1:
                terms = [terms[i] + terms[i + 1] for i in range(0, len(terms), 2)]
            tiles[t] = jnp.where(inside, 0.0, tiles[t]) - terms[0]
        if b < 6:
            b1, b2, b3 = split(jnp.concatenate(rows, axis=0))
            change = lax.dot_general(
                jnp.concatenate([a1, a1, a2, a2, a1, a3], axis=0),
                jnp.concatenate([b1, b2, b1, b2, b3, b1], axis=0),
                (((0,), (0,)), ((), ())),
                preferred_element_type=F,
            )
            for t in range(2 * b + 4, 16):
                tiles[t] = jnp.where(inside, 0.0, tiles[t]) - change[8 * t : 8 * t + 8]
    return out


def factor(g, rank):
    row=lax.broadcasted_iota(jnp.int32,(128,128),0); col=lax.broadcasted_iota(jnp.int32,(128,128),1)
    keep=(row.astype(F)<rank)&(col.astype(F)<rank)
    masked=jnp.where(keep,g,0.0)
    eye=row==col
    trace=jnp.sum(jnp.where(eye,masked,0.0),keepdims=True)
    delta=0.01*trace/rank
    a=masked*(1.0/delta)+jnp.where(eye,1.0,0.0)
    linv=jnp.concatenate(eliminate([a[8*t:8*t+8] for t in range(16)]),axis=0)
    linv=jnp.where(keep,linv*lax.rsqrt(delta),0.0)
    return masked, linv

def dot(a, b):
    return jnp.dot(a, b, precision=HIGHEST, preferred_element_type=F)


def dot_tn(a, b):
    return lax.dot_general(a, b, (((0,), (0,)), ((), ())), precision=HIGHEST, preferred_element_type=F)


def dot_nt(a, b):
    return lax.dot_general(a, b, (((1,), (1,)), ((), ())), precision=HIGHEST, preferred_element_type=F)


def partner_of(level, row_at, col_at):
    step = (level + 1) // 2
    odd = level % 2
    row = row_at + odd * step * (1 - 2 * ((row_at // step) % 2))
    col = col_at + (1 - odd) * step * (1 - 2 * ((col_at // step) % 2))
    return row, col


def combine(taps, pads):
    pads[...] = jnp.zeros_like(pads)
    for which in range(2):
        for dim in range(2):
            pads[which, dim : dim + 1, 0 : taps.shape[2]] = taps[dim, which : which + 1, :]
    first, second = pads[0], pads[1]
    total = jnp.zeros_like(first)
    for b in range(taps.shape[2]):
        moved = pltpu.roll(first, 4 * b, 1) if b else first
        total = total + moved * jnp.broadcast_to(second[:, b : b + 1], first.shape)
    return total.astype(BF)

def stretched(line, length, width):
    sub = lax.broadcasted_iota(jnp.int32, (8, width), 0)
    base = jnp.broadcast_to(line, (8, width))
    for bit in (1, 2, 4):
        base = jnp.where((sub // bit) % 2 == 1, pltpu.roll(base, bit, 1), base)
    tiles = [base] + [pltpu.roll(base, 8 * t, 1) for t in range(1, length // 8)]
    return jnp.concatenate(tiles, axis=0)


def body(
    taps, ranks, probes, sketch, weights_ref, moved_ref,
    tall, broad, mix, across, part, gram_ref, taps_ref, ranks_ref, pads, own, other, zeta_ref,
    small_sem, own_sem, row_send, row_recv, col_send, col_recv, swap_send, swap_recv,
):
    n_x, n_y = lax.axis_size("tx"), lax.axis_size("ty")
    row_at, col_at = lax.axis_index("tx"), lax.axis_index("ty")
    has_up, has_down = row_at > 0, row_at < n_x - 1
    has_left, has_right = col_at > 0, col_at < n_y - 1
    up, down = (row_at - 1, col_at), (row_at + 1, col_at)
    left, right = (row_at, col_at - 1), (row_at, col_at + 1)
    sides = ((has_up, up), (has_down, down), (has_left, left), (has_right, right))

    load = pltpu.make_async_copy(probes, tall.at[pl.ds(REACH, SIDE)], own_sem)
    load.start()
    small = [
        pltpu.make_async_copy(taps, taps_ref, small_sem.at[0]),
        pltpu.make_async_copy(ranks, ranks_ref, small_sem.at[1]),
    ]
    for copy in small:
        copy.start()
    barrier = pltpu.get_barrier_semaphore()
    for there, device in sides:
        @pl.when(there)
        def _():
            pl.semaphore_signal(barrier, inc=1, device_id=device, device_id_type=MESH)

    @pl.loop(1, 5)
    def _(level):
        pl.semaphore_signal(
            barrier, inc=1, device_id=partner_of(level, row_at, col_at), device_id_type=MESH
        )

    peers = [there.astype(jnp.int32) for there, _ in sides]
    pl.semaphore_wait(barrier, peers[0] + peers[1] + peers[2] + peers[3] + 4)

    def row_copy(to_down, step, first):
        count = 24 if first else 8
        far = 8 * step + 24
        if to_down:
            source, target, device, way = SIDE - far, REACH - far, down, 0
        else:
            source, target, device, way = far - count, REACH + SIDE + far - count, up, 1
        return pltpu.make_async_remote_copy(
            src_ref=probes.at[pl.ds(source, count)],
            dst_ref=tall.at[pl.ds(target, count)],
            send_sem=row_send.at[way, step],
            recv_sem=row_recv.at[way, step],
            device_id=device,
            device_id_type=MESH,
        )

    def col_copy(to_right, step, low):
        rows = 8 * (7 - step) if low else 8 * (8 + step)
        if to_right:
            source, target, device, way = SIDE, 0, right, 0
        else:
            source, target, device, way = REACH, REACH + SIDE, left, 1
        half = 0 if low else 1
        return pltpu.make_async_remote_copy(
            src_ref=broad.at[pl.ds(rows, 8), pl.ds(source, REACH)],
            dst_ref=broad.at[pl.ds(rows, 8), pl.ds(target, REACH)],
            send_sem=col_send.at[way, half, step],
            recv_sem=col_recv.at[way, half, step],
            device_id=device,
            device_id_type=MESH,
        )

    def each(action, step, first=False):
        for there, to_down in ((has_down, True), (has_up, False)):
            @pl.when(there)
            def _():
                action(row_copy(to_down, step, first))

    def each_arrival(step, first=False):
        for there, to_down in ((has_up, True), (has_down, False)):
            @pl.when(there)
            def _():
                row_copy(to_down, step, first).wait_recv()

    start = lambda copy: copy.start()
    sent = lambda copy: copy.wait_send()
    each(start, 0, True)
    each(start, 1)
    for copy in small:
        copy.wait()
    lines = combine(taps_ref, pads)
    wide = mix.shape[1]
    spot = lax.broadcasted_iota(jnp.int32, (256, wide), 1)
    spread = jnp.where(spot == 16 * lax.broadcasted_iota(jnp.int32, (256, wide), 0), 1.0, 0.0)
    line_x = jnp.dot(lines, spread.astype(BF), preferred_element_type=F)[0:1]
    line_y = jnp.concatenate([lines[1:2].astype(F), jnp.zeros((1, 128), F)], axis=1)
    mix[...] = stretched(line_x, 128, wide).astype(BF)
    across[...] = stretched(line_y, 128, across.shape[1]).astype(BF)

    @pl.when(jnp.logical_not(has_up))
    def _():
        tall[pl.ds(0, REACH)] = jnp.zeros((REACH, SIDE, SIDE), BF)

    @pl.when(jnp.logical_not(has_down))
    def _():
        tall[pl.ds(REACH + SIDE, REACH)] = jnp.zeros((REACH, SIDE, SIDE), BF)

    @pl.when(jnp.logical_not(has_left))
    def _():
        broad[:, pl.ds(0, REACH)] = jnp.zeros((SIDE, REACH, SIDE), BF)

    @pl.when(jnp.logical_not(has_right))
    def _():
        broad[:, pl.ds(REACH + SIDE, REACH)] = jnp.zeros((SIDE, REACH, SIDE), BF)

    gram_ref[...] = jnp.zeros_like(gram_ref)
    load.wait()

    def first_row(step, block):
        return pl.multiple_of(8 * (7 - step + block * (1 + 2 * step)), 8)

    def place(step, block, group):
        return 4 * block + group, first_row(step, block), 32 * group

    def aligned(cols):
        return cols if isinstance(cols, int) else pl.multiple_of(cols, 16)

    def columns(rows, depth, cols):
        return jnp.concatenate(
            [
                tall[pl.ds(rows, depth), pl.ds(aligned(cols + 16 * k), 16)].reshape(depth * 16, SIDE)
                for k in range(2)
            ],
            axis=1,
        )

    def begin_rows(step):
        @pl.loop(0, 4)
        def _(group):
            for block in range(2):
                index, rows, cols = place(step, block, group)
                near = 8 * (1 - block)
                part[index] = jnp.dot(
                    mix[:, 16 * near : 16 * near + 32 * REACH],
                    columns(rows + near, 2 * REACH, cols),
                    preferred_element_type=F,
                )

    def finish_rows(step):
        for block, group in [(block, group) for block in range(2) for group in range(4)]:
            index, rows, cols = place(step, block, group)
            far = 2 * REACH * block
            newest = columns(rows + far, 8, cols)
            middle = (
                part[index]
                + jnp.dot(mix[:, 16 * far : 16 * far + 128], newest, preferred_element_type=F)
            ).astype(BF)
            for k in range(2):
                broad[pl.ds(rows, 8), pl.ds(REACH + cols + 16 * k, 16)] = middle[
                    :, SIDE * k : SIDE * (k + 1)
                ].reshape(8, 16, SIDE)

    def send_cols(step):
        for there, to_right in ((has_right, True), (has_left, False)):
            for low in (True, False):
                @pl.when(there)
                def _():
                    col_copy(to_right, step, low).start()

    def filter_cols(step):
        for there, to_right in ((has_left, True), (has_right, False)):
            for low in (True, False):
                @pl.when(there)
                def _():
                    col_copy(to_right, step, low).wait_recv()

        for block in range(2):
            rows = first_row(step, block)
            for k in range(4):
                pair = [broad[rows + 2 * k + m] for m in range(2)]
                result = jnp.dot(
                    across[:, : SIDE + 2 * REACH],
                    jnp.concatenate(pair, axis=1),
                    preferred_element_type=F,
                ).astype(BF)
                for m in range(2):
                    sketch[rows + 2 * k + m] = result[:, SIDE * m : SIDE * (m + 1)]
            flat = sketch[pl.ds(rows, 8)].reshape(8 * SIDE, SIDE)
            gram_ref[...] += lax.dot_general(
                flat, flat, (((0,), (0,)), ((), ())), preferred_element_type=F
            )

    each_arrival(0, True)
    begin_rows(0)

    @pl.loop(0, STEPS)
    def _(step):
        @pl.when(step > 0)
        def _():
            each_arrival(step)
        finish_rows(step)
        send_cols(step)

        @pl.when(step == 0)
        def _():
            each(sent, 0, True)

        @pl.when(step > 0)
        def _():
            each(sent, step)

        @pl.when(step < STEPS - 2)
        def _():
            each(start, step + 2)

        @pl.when(step < STEPS - 1)
        def _():
            begin_rows(step + 1)

        @pl.when(step > 0)
        def _():
            filter_cols(step - 1)

    filter_cols(STEPS - 1)

    def swap(level):
        return pltpu.make_async_remote_copy(
            src_ref=own.at[level],
            dst_ref=other.at[level],
            send_sem=swap_send.at[level],
            recv_sem=swap_recv.at[level],
            device_id=partner_of(level, row_at, col_at),
            device_id_type=MESH,
        )

    def rank_at(level, row, col):
        table = ranks_ref[level]
        spot = (lax.broadcasted_iota(jnp.int32, table.shape, 0) == col) & (
            lax.broadcasted_iota(jnp.int32, table.shape, 1) == row
        )
        return jnp.sum(jnp.where(spot, table, 0).astype(F), keepdims=True)

    masked, linv = factor(gram_ref[...] * (1.0 / (SIDE * SIDE)), rank_at(0, row_at, col_at))
    zeta = dot(linv, masked)
    zeta_ref[...] = zeta
    own[1] = dot_tn(zeta, zeta)
    swap(1).start()
    weights_ref[...] = linv.T.astype(BF)

    @pl.loop(1, 5)
    def _(level):
        span_x = jnp.where(level < 3, 2, 4)
        span_y = jnp.where(level < 2, 1, jnp.where(level < 4, 2, 4))
        rank = rank_at(level, row_at - row_at % span_x, col_at - col_at % span_y)
        swap(level).wait_recv()
        masked, linv = factor((own[level] + other[level]) * 0.5, rank)
        child = zeta_ref[...]

        @pl.when(level < 4)
        def _():
            zeta = dot(linv, masked)
            zeta_ref[...] = zeta
            own[level + 1] = dot_tn(zeta, zeta)
            swap(level + 1).start()

        moved_ref[0, 0, level - 1] = dot_nt(child, linv)

    @pl.loop(1, 5)
    def _(level):
        swap(level).wait_send()

    @pl.loop(0, STEPS)
    def _(step):
        for there, to_right in ((has_right, True), (has_left, False)):
            for low in (True, False):
                @pl.when(there)
                def _():
                    col_copy(to_right, step, low).wait_send()


def compress(taps, ranks, probes):
    depth = 8 + 2 * REACH
    return pl.pallas_call(
        body,
        out_shape=(
            jax.ShapeDtypeStruct((SIDE, SIDE, SIDE), BF),
            jax.ShapeDtypeStruct((SIDE, SIDE), BF),
            jax.ShapeDtypeStruct((1, 1, 4, SIDE, SIDE), F),
        ),
        in_specs=[pl.BlockSpec(memory_space=pltpu.HBM)] * 3,
        out_specs=(pl.BlockSpec(memory_space=pltpu.VMEM),) * 3,
        scratch_shapes=[
            pltpu.VMEM((SIDE + 2 * REACH, SIDE, SIDE), BF),
            pltpu.VMEM((SIDE, SIDE + 2 * REACH, SIDE), BF),
            pltpu.VMEM((SIDE, 16 * depth), BF),
            pltpu.VMEM((SIDE, 384), BF),
            pltpu.VMEM((8, SIDE, 2 * SIDE), F),
            pltpu.VMEM((SIDE, SIDE), F),
            pltpu.VMEM(taps.shape, F),
            pltpu.VMEM(ranks.shape, jnp.int32),
            pltpu.VMEM((2, 16, 256), F),
            pltpu.VMEM((5, SIDE, SIDE), F),
            pltpu.VMEM((5, SIDE, SIDE), F),
            pltpu.VMEM((SIDE, SIDE), F),
            pltpu.SemaphoreType.DMA((2,)),
            pltpu.SemaphoreType.DMA,
            pltpu.SemaphoreType.DMA((2, STEPS)),
            pltpu.SemaphoreType.DMA((2, STEPS)),
            pltpu.SemaphoreType.DMA((2, 2, STEPS)),
            pltpu.SemaphoreType.DMA((2, 2, STEPS)),
            pltpu.SemaphoreType.DMA((5,)),
            pltpu.SemaphoreType.DMA((5,)),
        ],
        compiler_params=pltpu.CompilerParams(
            collective_id=0, has_side_effects=True, vmem_limit_bytes=48 * 2**20
        ),
        name="compress",
    )(taps, ranks, probes)


CHUNKS = 8


def basis_kernel(sketch, weights_ref, moved, out, moved_out, result, store_sem, pass_sem):
    rows = SIDE // CHUNKS

    def store(index):
        here = pl.ds(rows * index, rows)
        return pltpu.make_async_copy(result.at[here], out.at[here], store_sem.at[index])

    forward = pltpu.make_async_copy(moved, moved_out, pass_sem)
    forward.start()
    weights = weights_ref[...]
    zero = jnp.zeros_like(weights)
    twice = jnp.concatenate(
        [jnp.concatenate([weights, zero], axis=1), jnp.concatenate([zero, weights], axis=1)], axis=0
    )

    @pl.loop(0, CHUNKS)
    def _(index):
        half = rows // 2
        base = rows * index
        pair = [
            sketch[pl.ds(base + half * k, half)].reshape(half * SIDE, SIDE) for k in range(2)
        ]
        both = jnp.dot(jnp.concatenate(pair, axis=1), twice, preferred_element_type=F).astype(BF)
        for k in range(2):
            result[pl.ds(base + half * k, half)] = both[:, SIDE * k : SIDE * (k + 1)].reshape(
                half, SIDE, SIDE
            )
        store(index).start()

    for index in range(CHUNKS):
        store(index).wait()
    forward.wait()


def basis(sketch, weights, moved):
    return pl.pallas_call(
        basis_kernel,
        out_shape=(
            jax.ShapeDtypeStruct(sketch.shape, BF),
            jax.ShapeDtypeStruct(moved.shape, F),
        ),
        in_specs=[pl.BlockSpec(memory_space=pltpu.VMEM)] * 3,
        out_specs=(pl.BlockSpec(memory_space=pltpu.HBM),) * 2,
        scratch_shapes=[
            pltpu.VMEM(sketch.shape, BF),
            pltpu.SemaphoreType.DMA((CHUNKS,)),
            pltpu.SemaphoreType.DMA,
        ],
        compiler_params=pltpu.CompilerParams(vmem_limit_bytes=16 * 2**20),
        name="basis",
    )(sketch, weights, moved)


def local(probes, filter_taps, cluster_ranks):
    sketch, weights, moved = compress(filter_taps, jnp.swapaxes(cluster_ranks, 1, 2), probes)
    return basis(sketch, weights, moved)


def solution(mesh):
    in_specs = (P("tx", "ty", None), P(), P())
    out_specs = (P("tx", "ty", None), P("tx", "ty", None, None, None))
    return jax.shard_map(local, mesh=mesh, in_specs=in_specs, out_specs=out_specs, check_vma=False)
```

```python
import jax
import jax.numpy as jnp
from jax import lax
from jax.experimental import pallas as pl
from jax.experimental.pallas import tpu as pltpu
from jax.sharding import PartitionSpec as P

HIGHEST = lax.Precision.HIGHEST
F = jnp.float32
BF = jnp.bfloat16
REACH = 80
SIDE = 128
STEPS = 8
MESH = pl.DeviceIdType.MESH


def lane_of(x, i):
    return jnp.broadcast_to(x[:, i : i + 1], (8, 128))


def row_of(x, i):
    return jnp.broadcast_to(x[i : i + 1, :], (8, 128))


def split(a):
    one = a.astype(BF)
    rest = a - one.astype(F)
    two = rest.astype(BF)
    return one, two, (rest - two.astype(F)).astype(BF)


def eliminate(tiles, extra, emit):
    sub = lax.broadcasted_iota(jnp.int32, (8, 128), 0)
    lane = lax.broadcasted_iota(jnp.int32, (8, 128), 1)
    zero = jnp.zeros((8, 128), F)
    sets = [list(tiles)] + ([list(extra)] if extra is not None else [])
    tiles = sets[0]
    for b in range(8):
        j = 16 * b
        near = range(2 * b + 2, min(2 * b + 4, 16))
        body = [2 * b, 2 * b + 1, *near]
        cols = {
            t: [lane_of(tiles[t], j + c) if t > 2 * b or c < 8 else None for c in range(16)]
            for t in body
        }
        inside = (lane >= j) & (lane < j + 16)
        for t in body:
            h = t - 2 * b
            unit = jnp.where(lane - j == sub + 8 * h, 1.0, 0.0) if h < 2 else 0.0
            tiles[t] = jnp.where(inside, unit, tiles[t])
        kept = [[zero, zero] for _ in sets]
        raw, scaled = [zero, zero], [[zero, zero] for _ in sets]
        for c in range(16):
            h, s = divmod(c, 8)
            first = 2 * b + h
            pivot = row_of(cols[first][c], s)
            inv, root = 1.0 / pivot, lax.rsqrt(pivot)
            lines = [row_of(one[first], s) for one in sets]
            for k, line in enumerate(lines):
                kept[k][h] = jnp.where(sub == s, line * root, kept[k][h])
                if b < 6:
                    scaled[k][h] = jnp.where(sub == s, line * inv, scaled[k][h])
            if b < 6:
                raw[h] = jnp.where(sub == s, lines[0], raw[h])
            for t in body[h:]:
                ratio = cols[t][c] * inv
                for e in range(c + 1, 16):
                    if t >= 2 * b + e // 8:
                        entry = row_of(cols[2 * b + e // 8][c], e % 8)
                        cols[t][e] = cols[t][e] - ratio * entry
                for k, line in enumerate(lines):
                    sets[k][t] = sets[k][t] - ratio * line
        emit(
            b,
            [jnp.where(lane <= j + 8 * h + sub, kept[0][h], 0.0) for h in range(2)],
            kept[1] if len(sets) > 1 else None,
        )
        if b < 6:
            a1, a2, a3 = split(jnp.concatenate(raw, axis=0))
            wide = [jnp.concatenate(pair, axis=0) for pair in scaled]
            b1, b2, b3 = split(jnp.concatenate(wide, axis=1))
            change = lax.dot_general(
                jnp.concatenate([a1, a1, a2, a2, a1, a3], axis=0),
                jnp.concatenate([b1, b2, b1, b2, b3, b1], axis=0),
                (((0,), (0,)), ((), ())),
                preferred_element_type=F,
            )
            for t in range(2 * b + 4, 16):
                tiles[t] = jnp.where(inside, 0.0, tiles[t])
                for k, one in enumerate(sets):
                    one[t] = one[t] - change[8 * t : 8 * t + 8, 128 * k : 128 * k + 128]


def factor(gram, rank, emit=None):
    row = lax.broadcasted_iota(jnp.int32, (128, 128), 0)
    col = lax.broadcasted_iota(jnp.int32, (128, 128), 1)
    keep = (row < rank) & (col < rank)
    masked = jnp.where(keep, gram, 0.0)
    eye = row == col
    trace = jnp.sum(jnp.where(eye, masked, 0.0), keepdims=True)
    delta = 0.01 * trace / jnp.full((1, 1), rank, jnp.int32).astype(F)
    shifted = masked * (1.0 / delta) + jnp.where(eye, 1.0, 0.0)
    root = jnp.broadcast_to(lax.rsqrt(delta), (16, 128))
    out = []

    def take(b, inverse, solved):
        out.append(jnp.concatenate(inverse, axis=0) * root)
        if emit is not None:
            emit(b, jnp.concatenate(solved, axis=0) * root)

    def tiles(a):
        return [a[8 * t : 8 * t + 8] for t in range(16)]

    eliminate(tiles(shifted), tiles(masked) if emit is not None else None, take)
    return jnp.where(keep, jnp.concatenate(out, axis=0), 0.0)


def dot_tn(a, b):
    return lax.dot_general(a, b, (((0,), (0,)), ((), ())), precision=HIGHEST, preferred_element_type=F)


def dot_nt(a, b):
    return lax.dot_general(a, b, (((1,), (1,)), ((), ())), precision=HIGHEST, preferred_element_type=F)


def partner_of(level, row_at, col_at):
    step = (level + 1) // 2
    odd = level % 2
    row = row_at + odd * step * (1 - 2 * ((row_at // step) % 2))
    col = col_at + (1 - odd) * step * (1 - 2 * ((col_at // step) % 2))
    return row, col


def combine(taps):
    sub = lax.broadcasted_iota(jnp.int32, (16, 256), 0)
    lane = lax.broadcasted_iota(jnp.int32, (16, 256), 1)
    count = taps.shape[2]

    def of(which, index):
        return jnp.where(sub == 0, taps[0, which, index], taps[1, which, index])

    first = jnp.zeros((16, 256), F)
    for a in range(count):
        first = jnp.where(lane == a, of(0, a), first)
    total = jnp.zeros((16, 256), F)
    for b in range(count):
        total = total + (pltpu.roll(first, 4 * b, 1) if b else first) * of(1, b)
    return total.astype(BF)


def stretched(line, length, width):
    sub = lax.broadcasted_iota(jnp.int32, (8, width), 0)
    base = jnp.broadcast_to(line, (8, width))
    for bit in (1, 2, 4):
        base = jnp.where((sub // bit) % 2 == 1, pltpu.roll(base, bit, 1), base)
    tiles = [base] + [pltpu.roll(base, 8 * t, 1) for t in range(1, length // 8)]
    return jnp.concatenate(tiles, axis=0)


def body(
    taps, ranks, probes, sketch, weights_ref, moved_ref,
    tall, broad, mix, across, part, gram_ref, own, other,
    own_sem, row_send, row_recv, col_send, col_recv, swap_send, swap_recv,
):
    n_x, n_y = lax.axis_size("tx"), lax.axis_size("ty")
    row_at, col_at = lax.axis_index("tx"), lax.axis_index("ty")
    has_up, has_down = row_at > 0, row_at < n_x - 1
    has_left, has_right = col_at > 0, col_at < n_y - 1
    up, down = (row_at - 1, col_at), (row_at + 1, col_at)
    left, right = (row_at, col_at - 1), (row_at, col_at + 1)
    sides = ((has_up, up), (has_down, down), (has_left, left), (has_right, right))

    load = pltpu.make_async_copy(probes, tall.at[pl.ds(REACH, SIDE)], own_sem)
    load.start()
    barrier = pltpu.get_barrier_semaphore()
    for there, device in sides:
        @pl.when(there)
        def _():
            pl.semaphore_signal(barrier, inc=1, device_id=device, device_id_type=MESH)

    @pl.loop(1, 5)
    def _(level):
        pl.semaphore_signal(
            barrier, inc=1, device_id=partner_of(level, row_at, col_at), device_id_type=MESH
        )

    peers = [there.astype(jnp.int32) for there, _ in sides]
    pl.semaphore_wait(barrier, peers[0] + peers[1] + peers[2] + peers[3] + 4)

    def row_copy(to_down, step, first):
        count = 24 if first else 8
        far = 8 * step + 24
        if to_down:
            source, target, device, way = SIDE - far, REACH - far, down, 0
        else:
            source, target, device, way = far - count, REACH + SIDE + far - count, up, 1
        return pltpu.make_async_remote_copy(
            src_ref=probes.at[pl.ds(source, count)],
            dst_ref=tall.at[pl.ds(target, count)],
            send_sem=row_send.at[way, step],
            recv_sem=row_recv.at[way, step],
            device_id=device,
            device_id_type=MESH,
        )

    def col_copy(to_right, step, low):
        rows = 8 * (7 - step) if low else 8 * (8 + step)
        if to_right:
            source, target, device, way = SIDE, 0, right, 0
        else:
            source, target, device, way = REACH, REACH + SIDE, left, 1
        half = 0 if low else 1
        return pltpu.make_async_remote_copy(
            src_ref=broad.at[pl.ds(rows, 8), pl.ds(source, REACH)],
            dst_ref=broad.at[pl.ds(rows, 8), pl.ds(target, REACH)],
            send_sem=col_send.at[way, half, step],
            recv_sem=col_recv.at[way, half, step],
            device_id=device,
            device_id_type=MESH,
        )

    def each(action, step, first=False):
        for there, to_down in ((has_down, True), (has_up, False)):
            @pl.when(there)
            def _():
                action(row_copy(to_down, step, first))

    def each_arrival(step, first=False):
        for there, to_down in ((has_up, True), (has_down, False)):
            @pl.when(there)
            def _():
                row_copy(to_down, step, first).wait_recv()

    start = lambda copy: copy.start()
    sent = lambda copy: copy.wait_send()
    each(start, 0, True)
    each(start, 1)
    lines = combine(taps)
    wide = mix.shape[1]
    spot = lax.broadcasted_iota(jnp.int32, (256, wide), 1)
    spread = jnp.where(spot == 16 * lax.broadcasted_iota(jnp.int32, (256, wide), 0), 1.0, 0.0)
    line_x = jnp.dot(lines, spread.astype(BF), preferred_element_type=F)[0:1]
    line_y = jnp.concatenate([lines[1:2].astype(F), jnp.zeros((1, 128), F)], axis=1)
    mix[...] = stretched(line_x, 128, wide).astype(BF)
    across[...] = stretched(line_y, 128, across.shape[1]).astype(BF)

    @pl.when(jnp.logical_not(has_up))
    def _():
        tall[pl.ds(0, REACH)] = jnp.zeros((REACH, SIDE, SIDE), BF)

    @pl.when(jnp.logical_not(has_down))
    def _():
        tall[pl.ds(REACH + SIDE, REACH)] = jnp.zeros((REACH, SIDE, SIDE), BF)

    @pl.when(jnp.logical_not(has_left))
    def _():
        broad[:, pl.ds(0, REACH)] = jnp.zeros((SIDE, REACH, SIDE), BF)

    @pl.when(jnp.logical_not(has_right))
    def _():
        broad[:, pl.ds(REACH + SIDE, REACH)] = jnp.zeros((SIDE, REACH, SIDE), BF)

    gram_ref[...] = jnp.zeros_like(gram_ref)
    load.wait()

    def first_row(step, block):
        return pl.multiple_of(8 * (7 - step + block * (1 + 2 * step)), 8)

    def place(step, block, group):
        return 4 * block + group, first_row(step, block), 32 * group

    def aligned(cols):
        return cols if isinstance(cols, int) else pl.multiple_of(cols, 16)

    def columns(rows, depth, cols):
        return jnp.concatenate(
            [
                tall[pl.ds(rows, depth), pl.ds(aligned(cols + 16 * k), 16)].reshape(depth * 16, SIDE)
                for k in range(2)
            ],
            axis=1,
        )

    def begin_rows(step):
        @pl.loop(0, 4)
        def _(group):
            for block in range(2):
                index, rows, cols = place(step, block, group)
                near = 8 * (1 - block)
                part[index] = jnp.dot(
                    mix[:, 16 * near : 16 * near + 32 * REACH],
                    columns(rows + near, 2 * REACH, cols),
                    preferred_element_type=F,
                )

    def finish_rows(step):
        for block, group in [(block, group) for block in range(2) for group in range(4)]:
            index, rows, cols = place(step, block, group)
            far = 2 * REACH * block
            newest = columns(rows + far, 8, cols)
            middle = (
                part[index]
                + jnp.dot(mix[:, 16 * far : 16 * far + 128], newest, preferred_element_type=F)
            ).astype(BF)
            for k in range(2):
                broad[pl.ds(rows, 8), pl.ds(REACH + cols + 16 * k, 16)] = middle[
                    :, SIDE * k : SIDE * (k + 1)
                ].reshape(8, 16, SIDE)

    def send_cols(step):
        for there, to_right in ((has_right, True), (has_left, False)):
            for low in (True, False):
                @pl.when(there)
                def _():
                    col_copy(to_right, step, low).start()

    def filter_cols(step):
        for there, to_right in ((has_left, True), (has_right, False)):
            for low in (True, False):
                @pl.when(there)
                def _():
                    col_copy(to_right, step, low).wait_recv()

        for block in range(2):
            rows = first_row(step, block)
            for k in range(4):
                pair = [broad[rows + 2 * k + m] for m in range(2)]
                result = jnp.dot(
                    across[:, : SIDE + 2 * REACH],
                    jnp.concatenate(pair, axis=1),
                    preferred_element_type=F,
                ).astype(BF)
                for m in range(2):
                    sketch[rows + 2 * k + m] = result[:, SIDE * m : SIDE * (m + 1)]
            flat = sketch[pl.ds(rows, 8)].reshape(8 * SIDE, SIDE)
            gram_ref[...] += lax.dot_general(
                flat, flat, (((0,), (0,)), ((), ())), preferred_element_type=F
            )

    each_arrival(0, True)
    begin_rows(0)

    @pl.loop(0, STEPS)
    def _(step):
        @pl.when(step > 0)
        def _():
            each_arrival(step)
        finish_rows(step)
        send_cols(step)

        @pl.when(step == 0)
        def _():
            each(sent, 0, True)

        @pl.when(step > 0)
        def _():
            each(sent, step)

        @pl.when(step < STEPS - 2)
        def _():
            each(start, step + 2)

        @pl.when(step < STEPS - 1)
        def _():
            begin_rows(step + 1)

        @pl.when(step > 0)
        def _():
            filter_cols(step - 1)

    filter_cols(STEPS - 1)

    def swap(level, b):
        here = pl.ds(16 * b, 16)
        return pltpu.make_async_remote_copy(
            src_ref=own.at[level, here],
            dst_ref=other.at[level, here],
            send_sem=swap_send.at[level, b],
            recv_sem=swap_recv.at[level, b],
            device_id=partner_of(level + 1, row_at, col_at),
            device_id_type=MESH,
        )

    def rank_at(level, span_x, span_y):
        return ranks[level, col_at - col_at % span_y, row_at - row_at % span_x]

    gram_ref[...] = gram_ref[...] * (1.0 / (SIDE * SIDE))

    @pl.loop(0, 4)
    def _(level):
        span_x = jnp.where(level < 1, 1, jnp.where(level < 3, 2, 4))
        span_y = jnp.where(level < 2, 1, 2)

        def emit(b, solved):
            own[level, 16 * b : 16 * b + 16] = solved
            swap(level, b).start()

        linv = factor(gram_ref[...], rank_at(level, span_x, span_y), emit)

        @pl.when(level == 0)
        def _():
            weights_ref[...] = linv.T.astype(BF)

        @pl.when(level > 0)
        def _():
            moved_ref[0, 0, level - 1] = dot_nt(own[level - 1], linv)
        for b in range(8):
            swap(level, b).wait_recv()
        both = jnp.concatenate([own[level], other[level]], axis=0)
        gram_ref[...] = dot_tn(both, both) * 0.5

    linv = factor(gram_ref[...], rank_at(4, 4, 4))
    moved_ref[0, 0, 3] = dot_nt(own[3], linv)

    @pl.loop(0, 4)
    def _(level):
        for b in range(8):
            swap(level, b).wait_send()

    @pl.loop(0, STEPS)
    def _(step):
        for there, to_right in ((has_right, True), (has_left, False)):
            for low in (True, False):
                @pl.when(there)
                def _():
                    col_copy(to_right, step, low).wait_send()


def compress(taps, ranks, probes):
    depth = 8 + 2 * REACH
    return pl.pallas_call(
        body,
        out_shape=(
            jax.ShapeDtypeStruct((SIDE, SIDE, SIDE), BF),
            jax.ShapeDtypeStruct((SIDE, SIDE), BF),
            jax.ShapeDtypeStruct((1, 1, 4, SIDE, SIDE), F),
        ),
        in_specs=[
            pl.BlockSpec(memory_space=pltpu.SMEM),
            pl.BlockSpec(memory_space=pltpu.SMEM),
            pl.BlockSpec(memory_space=pltpu.HBM),
        ],
        out_specs=(pl.BlockSpec(memory_space=pltpu.VMEM),) * 3,
        scratch_shapes=[
            pltpu.VMEM((SIDE + 2 * REACH, SIDE, SIDE), BF),
            pltpu.VMEM((SIDE, SIDE + 2 * REACH, SIDE), BF),
            pltpu.VMEM((SIDE, 16 * depth), BF),
            pltpu.VMEM((SIDE, 384), BF),
            pltpu.VMEM((8, SIDE, 2 * SIDE), F),
            pltpu.VMEM((SIDE, SIDE), F),
            pltpu.VMEM((4, SIDE, SIDE), F),
            pltpu.VMEM((4, SIDE, SIDE), F),
            pltpu.SemaphoreType.DMA,
            pltpu.SemaphoreType.DMA((2, STEPS)),
            pltpu.SemaphoreType.DMA((2, STEPS)),
            pltpu.SemaphoreType.DMA((2, 2, STEPS)),
            pltpu.SemaphoreType.DMA((2, 2, STEPS)),
            pltpu.SemaphoreType.DMA((4, 8)),
            pltpu.SemaphoreType.DMA((4, 8)),
        ],
        compiler_params=pltpu.CompilerParams(
            collective_id=0, has_side_effects=True, vmem_limit_bytes=48 * 2**20
        ),
        name="compress",
    )(taps, ranks, probes)


CHUNKS = 8


def basis_kernel(sketch, weights_ref, moved, out, moved_out, result, store_sem, pass_sem):
    rows = SIDE // CHUNKS

    def store(index):
        here = pl.ds(rows * index, rows)
        return pltpu.make_async_copy(result.at[here], out.at[here], store_sem.at[index])

    forward = pltpu.make_async_copy(moved, moved_out, pass_sem)
    forward.start()
    weights = weights_ref[...]
    zero = jnp.zeros_like(weights)
    twice = jnp.concatenate(
        [jnp.concatenate([weights, zero], axis=1), jnp.concatenate([zero, weights], axis=1)], axis=0
    )

    @pl.loop(0, CHUNKS)
    def _(index):
        half = rows // 2
        base = rows * index
        pair = [
            sketch[pl.ds(base + half * k, half)].reshape(half * SIDE, SIDE) for k in range(2)
        ]
        both = jnp.dot(jnp.concatenate(pair, axis=1), twice, preferred_element_type=F).astype(BF)
        for k in range(2):
            result[pl.ds(base + half * k, half)] = both[:, SIDE * k : SIDE * (k + 1)].reshape(
                half, SIDE, SIDE
            )
        store(index).start()

    for index in range(CHUNKS):
        store(index).wait()
    forward.wait()


def basis(sketch, weights, moved):
    return pl.pallas_call(
        basis_kernel,
        out_shape=(
            jax.ShapeDtypeStruct(sketch.shape, BF),
            jax.ShapeDtypeStruct(moved.shape, F),
        ),
        in_specs=[pl.BlockSpec(memory_space=pltpu.VMEM)] * 3,
        out_specs=(pl.BlockSpec(memory_space=pltpu.HBM),) * 2,
        scratch_shapes=[
            pltpu.VMEM(sketch.shape, BF),
            pltpu.SemaphoreType.DMA((CHUNKS,)),
            pltpu.SemaphoreType.DMA,
        ],
        compiler_params=pltpu.CompilerParams(vmem_limit_bytes=16 * 2**20),
        name="basis",
    )(sketch, weights, moved)


def local(probes, filter_taps, cluster_ranks):
    sketch, weights, moved = compress(filter_taps, jnp.swapaxes(cluster_ranks, 1, 2), probes)
    return basis(sketch, weights, moved)


def solution(mesh):
    in_specs = (P("tx", "ty", None), P(), P())
    out_specs = (P("tx", "ty", None), P("tx", "ty", None, None, None))
    return jax.shard_map(local, mesh=mesh, in_specs=in_specs, out_specs=out_specs, check_vma=False)
```

```python
import jax
import jax.numpy as jnp
from jax import lax
from jax.experimental import pallas as pl
from jax.experimental.pallas import tpu as pltpu
from jax.sharding import PartitionSpec as P

HIGHEST = lax.Precision.HIGHEST
F = jnp.float32
BF = jnp.bfloat16
REACH = 80
SIDE = 128
STEPS = 8
MESH = pl.DeviceIdType.MESH


def lane_of(x, i):
    return jnp.broadcast_to(x[:, i : i + 1], (8, 128))


def row_of(x, i):
    return jnp.broadcast_to(x[i : i + 1, :], (8, 128))


def split(a):
    one = a.astype(BF)
    rest = a - one.astype(F)
    two = rest.astype(BF)
    return one, two, (rest - two.astype(F)).astype(BF)


def eliminate(tiles, extra, emit):
    sub = lax.broadcasted_iota(jnp.int32, (8, 128), 0)
    lane = lax.broadcasted_iota(jnp.int32, (8, 128), 1)
    zero = jnp.zeros((8, 128), F)
    sets = [list(tiles)] + ([list(extra)] if extra is not None else [])
    tiles = sets[0]
    for b in range(8):
        j = 16 * b
        near = range(2 * b + 2, min(2 * b + 4, 16))
        body = [2 * b, 2 * b + 1, *near]
        cols = {
            t: [lane_of(tiles[t], j + c) if t > 2 * b or c < 8 else None for c in range(16)]
            for t in body
        }
        inside = (lane >= j) & (lane < j + 16)
        for t in body:
            h = t - 2 * b
            unit = jnp.where(lane - j == sub + 8 * h, 1.0, 0.0) if h < 2 else 0.0
            tiles[t] = jnp.where(inside, unit, tiles[t])
        kept = [[zero, zero] for _ in sets]
        raw, scaled = [zero, zero], [[zero, zero] for _ in sets]
        for c in range(16):
            h, s = divmod(c, 8)
            first = 2 * b + h
            pivot = row_of(cols[first][c], s)
            inv, root = 1.0 / pivot, lax.rsqrt(pivot)
            lines = [row_of(one[first], s) for one in sets]
            for k, line in enumerate(lines):
                kept[k][h] = jnp.where(sub == s, line * root, kept[k][h])
                if b < 6:
                    scaled[k][h] = jnp.where(sub == s, line * inv, scaled[k][h])
            if b < 6:
                raw[h] = jnp.where(sub == s, lines[0], raw[h])
            for t in body[h:]:
                ratio = cols[t][c] * inv
                for e in range(c + 1, 16):
                    if t >= 2 * b + e // 8:
                        entry = row_of(cols[2 * b + e // 8][c], e % 8)
                        cols[t][e] = cols[t][e] - ratio * entry
                for k, line in enumerate(lines):
                    sets[k][t] = sets[k][t] - ratio * line
        emit(
            b,
            [jnp.where(lane <= j + 8 * h + sub, kept[0][h], 0.0) for h in range(2)],
            kept[1] if len(sets) > 1 else None,
        )
        if b < 6:
            a1, a2, a3 = split(jnp.concatenate(raw, axis=0))
            wide = [jnp.concatenate(pair, axis=0) for pair in scaled]
            b1, b2, b3 = split(jnp.concatenate(wide, axis=1))
            change = lax.dot_general(
                jnp.concatenate([a1, a1, a2, a2, a1, a3], axis=0),
                jnp.concatenate([b1, b2, b1, b2, b3, b1], axis=0),
                (((0,), (0,)), ((), ())),
                preferred_element_type=F,
            )
            for t in range(2 * b + 4, 16):
                tiles[t] = jnp.where(inside, 0.0, tiles[t])
                for k, one in enumerate(sets):
                    one[t] = one[t] - change[8 * t : 8 * t + 8, 128 * k : 128 * k + 128]


def factor(gram, rank, emit=None):
    row = lax.broadcasted_iota(jnp.int32, (128, 128), 0)
    col = lax.broadcasted_iota(jnp.int32, (128, 128), 1)
    keep = (row < rank) & (col < rank)
    masked = jnp.where(keep, gram, 0.0)
    eye = row == col
    trace = jnp.sum(jnp.where(eye, masked, 0.0), keepdims=True)
    delta = 0.01 * trace / jnp.full((1, 1), rank, jnp.int32).astype(F)
    shifted = masked * (1.0 / delta) + jnp.where(eye, 1.0, 0.0)
    root = jnp.broadcast_to(lax.rsqrt(delta), (16, 128))
    out = []

    def take(b, inverse, solved):
        out.append(jnp.concatenate(inverse, axis=0) * root)
        if emit is not None:
            emit(b, jnp.concatenate(solved, axis=0) * root)

    def tiles(a):
        return [a[8 * t : 8 * t + 8] for t in range(16)]

    eliminate(tiles(shifted), tiles(masked) if emit is not None else None, take)
    return jnp.where(keep, jnp.concatenate(out, axis=0), 0.0)


def dot_tn(a, b):
    return lax.dot_general(a, b, (((0,), (0,)), ((), ())), precision=HIGHEST, preferred_element_type=F)


def dot_nt(a, b):
    return lax.dot_general(a, b, (((1,), (1,)), ((), ())), precision=HIGHEST, preferred_element_type=F)


def partner_of(level, row_at, col_at):
    step = (level + 1) // 2
    odd = level % 2
    row = row_at + odd * step * (1 - 2 * ((row_at // step) % 2))
    col = col_at + (1 - odd) * step * (1 - 2 * ((col_at // step) % 2))
    return row, col


def combine(taps):
    sub = lax.broadcasted_iota(jnp.int32, (16, 256), 0)
    lane = lax.broadcasted_iota(jnp.int32, (16, 256), 1)
    count = taps.shape[2]

    def of(which, index):
        return jnp.where(sub == 0, taps[0, which, index], taps[1, which, index])

    first = jnp.zeros((16, 256), F)
    for a in range(count):
        first = jnp.where(lane == a, of(0, a), first)
    total = jnp.zeros((16, 256), F)
    for b in range(count):
        total = total + (pltpu.roll(first, 4 * b, 1) if b else first) * of(1, b)
    return total.astype(BF)


def stretched(line, length, width):
    sub = lax.broadcasted_iota(jnp.int32, (8, width), 0)
    base = jnp.broadcast_to(line, (8, width))
    for bit in (1, 2, 4):
        base = jnp.where((sub // bit) % 2 == 1, pltpu.roll(base, bit, 1), base)
    tiles = [base] + [pltpu.roll(base, 8 * t, 1) for t in range(1, length // 8)]
    return jnp.concatenate(tiles, axis=0)


def body(
    taps_far, ranks_far, probes, sketch, weights_ref, moved_ref,
    tall, broad, mix, across, part, gram_ref, own, other, taps, ranks,
    small_sem, own_sem, row_send, row_recv, col_send, col_recv, swap_send, swap_recv,
):
    n_x, n_y = lax.axis_size("tx"), lax.axis_size("ty")
    row_at, col_at = lax.axis_index("tx"), lax.axis_index("ty")
    has_up, has_down = row_at > 0, row_at < n_x - 1
    has_left, has_right = col_at > 0, col_at < n_y - 1
    up, down = (row_at - 1, col_at), (row_at + 1, col_at)
    left, right = (row_at, col_at - 1), (row_at, col_at + 1)
    sides = ((has_up, up), (has_down, down), (has_left, left), (has_right, right))

    load = pltpu.make_async_copy(probes, tall.at[pl.ds(REACH, SIDE)], own_sem)
    load.start()
    small = [
        pltpu.make_async_copy(taps_far, taps, small_sem.at[0]),
        pltpu.make_async_copy(ranks_far, ranks, small_sem.at[1]),
    ]
    for copy in small:
        copy.start()
    barrier = pltpu.get_barrier_semaphore()
    for there, device in sides:
        @pl.when(there)
        def _():
            pl.semaphore_signal(barrier, inc=1, device_id=device, device_id_type=MESH)

    @pl.loop(1, 5)
    def _(level):
        pl.semaphore_signal(
            barrier, inc=1, device_id=partner_of(level, row_at, col_at), device_id_type=MESH
        )

    peers = [there.astype(jnp.int32) for there, _ in sides]
    pl.semaphore_wait(barrier, peers[0] + peers[1] + peers[2] + peers[3] + 4)

    def is_last(step):
        return isinstance(step, int) and step >= STEPS - 1

    def size_of(step):
        return 4 if is_last(step) else 8

    def first_row(step, block):
        if is_last(step):
            return (4, 120)[block] if step == STEPS - 1 else (0, 124)[block]
        return pl.multiple_of(8 * (7 - step + block * (1 + 2 * step)), 8)

    def row_copy(to_down, step, first):
        count = 24 if first else size_of(step)
        far = 48 + 4 * step if is_last(step) else 8 * step + 24
        if to_down:
            source, target, device, way = SIDE - far, REACH - far, down, 0
        else:
            source, target, device, way = far - count, REACH + SIDE + far - count, up, 1
        return pltpu.make_async_remote_copy(
            src_ref=probes.at[pl.ds(source, count)],
            dst_ref=tall.at[pl.ds(target, count)],
            send_sem=row_send.at[way, step],
            recv_sem=row_recv.at[way, step],
            device_id=device,
            device_id_type=MESH,
        )

    def col_copy(to_right, step, low):
        rows, count = first_row(step, 0 if low else 1), size_of(step)
        if to_right:
            source, target, device, way = SIDE, 0, right, 0
        else:
            source, target, device, way = REACH, REACH + SIDE, left, 1
        half = 0 if low else 1
        return pltpu.make_async_remote_copy(
            src_ref=broad.at[pl.ds(rows, count), pl.ds(source, REACH)],
            dst_ref=broad.at[pl.ds(rows, count), pl.ds(target, REACH)],
            send_sem=col_send.at[way, half, step],
            recv_sem=col_recv.at[way, half, step],
            device_id=device,
            device_id_type=MESH,
        )

    def each(action, step, first=False):
        for there, to_down in ((has_down, True), (has_up, False)):
            @pl.when(there)
            def _():
                action(row_copy(to_down, step, first))

    def each_arrival(step, first=False):
        for there, to_down in ((has_up, True), (has_down, False)):
            @pl.when(there)
            def _():
                row_copy(to_down, step, first).wait_recv()

    start = lambda copy: copy.start()
    sent = lambda copy: copy.wait_send()
    each(start, 0, True)
    each(start, 1)
    for copy in small:
        copy.wait()
    lines = combine(taps)
    wide = mix.shape[1]
    spot = lax.broadcasted_iota(jnp.int32, (256, wide), 1)
    spread = jnp.where(spot == 16 * lax.broadcasted_iota(jnp.int32, (256, wide), 0), 1.0, 0.0)
    line_x = jnp.dot(lines, spread.astype(BF), preferred_element_type=F)[0:1]
    line_y = jnp.concatenate([lines[1:2].astype(F), jnp.zeros((1, 128), F)], axis=1)
    mix[...] = stretched(line_x, 128, wide).astype(BF)
    across[...] = stretched(line_y, 128, across.shape[1]).astype(BF)

    @pl.when(jnp.logical_not(has_up))
    def _():
        tall[pl.ds(0, REACH)] = jnp.zeros((REACH, SIDE, SIDE), BF)

    @pl.when(jnp.logical_not(has_down))
    def _():
        tall[pl.ds(REACH + SIDE, REACH)] = jnp.zeros((REACH, SIDE, SIDE), BF)

    @pl.when(jnp.logical_not(has_left))
    def _():
        broad[:, pl.ds(0, REACH)] = jnp.zeros((SIDE, REACH, SIDE), BF)

    @pl.when(jnp.logical_not(has_right))
    def _():
        broad[:, pl.ds(REACH + SIDE, REACH)] = jnp.zeros((SIDE, REACH, SIDE), BF)

    gram_ref[...] = jnp.zeros_like(gram_ref)
    load.wait()

    def place(step, block, group):
        rows = pl.multiple_of(8 * (7 - step + block * (1 + 2 * step)), 8)
        return 4 * block + group, rows, 32 * group

    def aligned(cols):
        return cols if isinstance(cols, int) else pl.multiple_of(cols, 16)

    def columns(rows, depth, cols):
        return jnp.concatenate(
            [
                tall[pl.ds(rows, depth), pl.ds(aligned(cols + 16 * k), 16)].reshape(depth * 16, SIDE)
                for k in range(2)
            ],
            axis=1,
        )

    def begin_rows(step):
        @pl.loop(0, 4)
        def _(group):
            for block in range(2):
                index, rows, cols = place(step, block, group)
                near = 8 * (1 - block)
                part[index] = jnp.dot(
                    mix[:, 16 * near : 16 * near + 32 * REACH],
                    columns(rows + near, 2 * REACH, cols),
                    preferred_element_type=F,
                )

    def finish_rows(step):
        for block, group in [(block, group) for block in range(2) for group in range(4)]:
            index, rows, cols = place(step, block, group)
            far = 2 * REACH * block
            newest = columns(rows + far, 8, cols)
            middle = (
                part[index]
                + jnp.dot(mix[:, 16 * far : 16 * far + 128], newest, preferred_element_type=F)
            ).astype(BF)
            for k in range(2):
                broad[pl.ds(rows, 8), pl.ds(REACH + cols + 16 * k, 16)] = middle[
                    :, SIDE * k : SIDE * (k + 1)
                ].reshape(8, 16, SIDE)

    def finish_last(step):
        second = step == STEPS
        for block, group in [(block, group) for block in range(2) for group in range(4)]:
            depth = 8 if second else 4
            half = 64 * (second == (block == 1))
            start_row = 0 if block == 0 else REACH + SIDE + REACH - 8
            shift = 0 if second or block == 1 else 4
            offset = 16 * (2 * REACH * block + shift)
            newest = columns(start_row + shift, depth, 32 * group)
            middle = (
                part[4 * block + group, half : half + 64]
                + jnp.dot(
                    mix[half : half + 64, offset : offset + 16 * depth],
                    newest,
                    preferred_element_type=F,
                )
            ).astype(BF)
            rows = first_row(step, block)
            for k in range(2):
                broad[pl.ds(rows, 4), pl.ds(REACH + 32 * group + 16 * k, 16)] = middle[
                    :, SIDE * k : SIDE * (k + 1)
                ].reshape(4, 16, SIDE)

    def send_cols(step):
        for there, to_right in ((has_right, True), (has_left, False)):
            for low in (True, False):
                @pl.when(there)
                def _():
                    col_copy(to_right, step, low).start()

    def filter_cols(step):
        for there, to_right in ((has_left, True), (has_right, False)):
            for low in (True, False):
                @pl.when(there)
                def _():
                    col_copy(to_right, step, low).wait_recv()

        for block in range(2):
            rows = first_row(step, block)
            for k in range(size_of(step) // 2):
                pair = [broad[rows + 2 * k + m] for m in range(2)]
                result = jnp.dot(
                    across[:, : SIDE + 2 * REACH],
                    jnp.concatenate(pair, axis=1),
                    preferred_element_type=F,
                ).astype(BF)
                for m in range(2):
                    sketch[rows + 2 * k + m] = result[:, SIDE * m : SIDE * (m + 1)]
            flat = sketch[pl.ds(rows, size_of(step))].reshape(size_of(step) * SIDE, SIDE)
            gram_ref[...] += lax.dot_general(
                flat, flat, (((0,), (0,)), ((), ())), preferred_element_type=F
            )

    each_arrival(0, True)
    begin_rows(0)

    @pl.loop(0, STEPS - 1)
    def _(step):
        @pl.when(step > 0)
        def _():
            each_arrival(step)
        finish_rows(step)
        send_cols(step)

        @pl.when(step == 0)
        def _():
            each(sent, 0, True)

        @pl.when(step > 0)
        def _():
            each(sent, step)

        @pl.when(step < STEPS - 3)
        def _():
            each(start, step + 2)

        @pl.when(step == STEPS - 3)
        def _():
            each(start, STEPS - 1)

        @pl.when(step == STEPS - 2)
        def _():
            each(start, STEPS)

        begin_rows(step + 1)

        @pl.when(step > 0)
        def _():
            filter_cols(step - 1)

    last = (STEPS - 1, STEPS)
    for step in last:
        each_arrival(step)
        finish_last(step)
        send_cols(step)
        if step == last[0]:
            filter_cols(jnp.int32(STEPS - 2))
    for step in last:
        filter_cols(step)
        each(sent, step)

    def swap(level, b):
        here = pl.ds(16 * b, 16)
        return pltpu.make_async_remote_copy(
            src_ref=own.at[level, here],
            dst_ref=other.at[level, here],
            send_sem=swap_send.at[level, b],
            recv_sem=swap_recv.at[level, b],
            device_id=partner_of(level + 1, row_at, col_at),
            device_id_type=MESH,
        )

    def rank_at(level, span_x, span_y):
        return ranks[level, col_at - col_at % span_y, row_at - row_at % span_x]

    gram_ref[...] = gram_ref[...] * (1.0 / (SIDE * SIDE))

    @pl.loop(0, 4)
    def _(level):
        span_x = jnp.where(level < 1, 1, jnp.where(level < 3, 2, 4))
        span_y = jnp.where(level < 2, 1, 2)

        def emit(b, solved):
            own[level, 16 * b : 16 * b + 16] = solved
            swap(level, b).start()

        linv = factor(gram_ref[...], rank_at(level, span_x, span_y), emit)

        @pl.when(level == 0)
        def _():
            weights_ref[...] = linv.T.astype(BF)

        @pl.when(level > 0)
        def _():
            moved_ref[0, 0, level - 1] = dot_nt(own[level - 1], linv)
        for b in range(8):
            swap(level, b).wait_recv()
        both = jnp.concatenate([own[level], other[level]], axis=0)
        gram_ref[...] = dot_tn(both, both) * 0.5

    linv = factor(gram_ref[...], rank_at(4, 4, 4))
    moved_ref[0, 0, 3] = dot_nt(own[3], linv)

    @pl.loop(0, 4)
    def _(level):
        for b in range(8):
            swap(level, b).wait_send()

    def sent_cols(step):
        for there, to_right in ((has_right, True), (has_left, False)):
            for low in (True, False):
                @pl.when(there)
                def _():
                    col_copy(to_right, step, low).wait_send()

    @pl.loop(0, STEPS - 1)
    def _(step):
        sent_cols(step)

    for step in last:
        sent_cols(step)


def compress(taps, ranks, probes):
    depth = 8 + 2 * REACH
    return pl.pallas_call(
        body,
        out_shape=(
            jax.ShapeDtypeStruct((SIDE, SIDE, SIDE), BF),
            jax.ShapeDtypeStruct((SIDE, SIDE), BF),
            jax.ShapeDtypeStruct((1, 1, 4, SIDE, SIDE), F),
        ),
        in_specs=[
            pl.BlockSpec(memory_space=pltpu.HBM),
            pl.BlockSpec(memory_space=pltpu.HBM),
            pl.BlockSpec(memory_space=pltpu.HBM),
        ],
        out_specs=(pl.BlockSpec(memory_space=pltpu.VMEM),) * 3,
        scratch_shapes=[
            pltpu.VMEM((SIDE + 2 * REACH, SIDE, SIDE), BF),
            pltpu.VMEM((SIDE, SIDE + 2 * REACH, SIDE), BF),
            pltpu.VMEM((SIDE, 16 * depth), BF),
            pltpu.VMEM((SIDE, 384), BF),
            pltpu.VMEM((8, SIDE, 2 * SIDE), F),
            pltpu.VMEM((SIDE, SIDE), F),
            pltpu.VMEM((4, SIDE, SIDE), F),
            pltpu.VMEM((4, SIDE, SIDE), F),
            pltpu.SMEM(taps.shape, F),
            pltpu.SMEM(ranks.shape, jnp.int32),
            pltpu.SemaphoreType.DMA((2,)),
            pltpu.SemaphoreType.DMA,
            pltpu.SemaphoreType.DMA((2, STEPS + 1)),
            pltpu.SemaphoreType.DMA((2, STEPS + 1)),
            pltpu.SemaphoreType.DMA((2, 2, STEPS + 1)),
            pltpu.SemaphoreType.DMA((2, 2, STEPS + 1)),
            pltpu.SemaphoreType.DMA((4, 8)),
            pltpu.SemaphoreType.DMA((4, 8)),
        ],
        compiler_params=pltpu.CompilerParams(
            collective_id=0, has_side_effects=True, vmem_limit_bytes=48 * 2**20
        ),
        name="compress",
    )(*[pltpu.with_memory_space_constraint(a, pltpu.HBM) for a in (taps, ranks)], probes)


CHUNKS = 8


def basis_kernel(sketch, weights_ref, moved, out, moved_out, result, store_sem, pass_sem):
    rows = SIDE // CHUNKS

    def store(index):
        here = pl.ds(rows * index, rows)
        return pltpu.make_async_copy(result.at[here], out.at[here], store_sem.at[index])

    forward = pltpu.make_async_copy(moved, moved_out, pass_sem)
    forward.start()
    weights = weights_ref[...]
    zero = jnp.zeros_like(weights)
    twice = jnp.concatenate(
        [jnp.concatenate([weights, zero], axis=1), jnp.concatenate([zero, weights], axis=1)], axis=0
    )

    @pl.loop(0, CHUNKS)
    def _(index):
        half = rows // 2
        base = rows * index
        pair = [
            sketch[pl.ds(base + half * k, half)].reshape(half * SIDE, SIDE) for k in range(2)
        ]
        both = jnp.dot(jnp.concatenate(pair, axis=1), twice, preferred_element_type=F).astype(BF)
        for k in range(2):
            result[pl.ds(base + half * k, half)] = both[:, SIDE * k : SIDE * (k + 1)].reshape(
                half, SIDE, SIDE
            )
        store(index).start()

    for index in range(CHUNKS):
        store(index).wait()
    forward.wait()


def basis(sketch, weights, moved):
    return pl.pallas_call(
        basis_kernel,
        out_shape=(
            jax.ShapeDtypeStruct(sketch.shape, BF),
            jax.ShapeDtypeStruct(moved.shape, F),
        ),
        in_specs=[pl.BlockSpec(memory_space=pltpu.VMEM)] * 3,
        out_specs=(pl.BlockSpec(memory_space=pltpu.HBM),) * 2,
        scratch_shapes=[
            pltpu.VMEM(sketch.shape, BF),
            pltpu.SemaphoreType.DMA((CHUNKS,)),
            pltpu.SemaphoreType.DMA,
        ],
        compiler_params=pltpu.CompilerParams(vmem_limit_bytes=16 * 2**20),
        name="basis",
    )(sketch, weights, moved)


def local(probes, filter_taps, cluster_ranks):
    sketch, weights, moved = compress(filter_taps, jnp.swapaxes(cluster_ranks, 1, 2), probes)
    return basis(sketch, weights, moved)


def solution(mesh):
    in_specs = (P("tx", "ty", None), P(), P())
    out_specs = (P("tx", "ty", None), P("tx", "ty", None, None, None))
    return jax.shard_map(local, mesh=mesh, in_specs=in_specs, out_specs=out_specs, check_vma=False)
```

```python
import jax
import jax.numpy as jnp
from jax import lax
from jax.experimental import pallas as pl
from jax.experimental.pallas import tpu as pltpu
from jax.sharding import PartitionSpec as P

HIGHEST = lax.Precision.HIGHEST
F = jnp.float32
BF = jnp.bfloat16
REACH = 80
SIDE = 128
STEPS = 8
MESH = pl.DeviceIdType.MESH


def lane_of(x, i):
    return jnp.broadcast_to(x[:, i : i + 1], (8, 128))


def row_of(x, i):
    return jnp.broadcast_to(x[i : i + 1, :], (8, 128))


def split(a):
    one = a.astype(BF)
    rest = a - one.astype(F)
    two = rest.astype(BF)
    return one, two, (rest - two.astype(F)).astype(BF)


def eliminate(tiles, extra, emit):
    sub = lax.broadcasted_iota(jnp.int32, (8, 128), 0)
    lane = lax.broadcasted_iota(jnp.int32, (8, 128), 1)
    zero = jnp.zeros((8, 128), F)
    sets = [list(tiles)] + ([list(extra)] if extra is not None else [])
    tiles = sets[0]
    for b in range(8):
        j = 16 * b
        near = range(2 * b + 2, min(2 * b + 4, 16))
        body = [2 * b, 2 * b + 1, *near]
        cols = {
            t: [lane_of(tiles[t], j + c) if t > 2 * b or c < 8 else None for c in range(16)]
            for t in body
        }
        inside = (lane >= j) & (lane < j + 16)
        for t in body:
            h = t - 2 * b
            unit = jnp.where(lane - j == sub + 8 * h, 1.0, 0.0) if h < 2 else 0.0
            tiles[t] = jnp.where(inside, unit, tiles[t])
        kept = [[zero, zero] for _ in sets]
        raw, scaled = [zero, zero], [[zero, zero] for _ in sets]
        for c in range(16):
            h, s = divmod(c, 8)
            first = 2 * b + h
            pivot = row_of(cols[first][c], s)
            inv, root = 1.0 / pivot, lax.rsqrt(pivot)
            lines = [row_of(one[first], s) for one in sets]
            for k, line in enumerate(lines):
                kept[k][h] = jnp.where(sub == s, line * root, kept[k][h])
                if b < 6:
                    scaled[k][h] = jnp.where(sub == s, line * inv, scaled[k][h])
            if b < 6:
                raw[h] = jnp.where(sub == s, lines[0], raw[h])
            for t in body[h:]:
                ratio = cols[t][c] * inv
                for e in range(c + 1, 16):
                    if t >= 2 * b + e // 8:
                        entry = row_of(cols[2 * b + e // 8][c], e % 8)
                        cols[t][e] = cols[t][e] - ratio * entry
                for k, line in enumerate(lines):
                    sets[k][t] = sets[k][t] - ratio * line
        emit(
            b,
            [jnp.where(lane <= j + 8 * h + sub, kept[0][h], 0.0) for h in range(2)],
            kept[1] if len(sets) > 1 else None,
        )
        if b < 6:
            a1, a2, a3 = split(jnp.concatenate(raw, axis=0))
            wide = [jnp.concatenate(pair, axis=0) for pair in scaled]
            b1, b2, b3 = split(jnp.concatenate(wide, axis=1))
            change = lax.dot_general(
                jnp.concatenate([a1, a1, a2, a2, a1, a3], axis=0),
                jnp.concatenate([b1, b2, b1, b2, b3, b1], axis=0),
                (((0,), (0,)), ((), ())),
                preferred_element_type=F,
            )
            for t in range(2 * b + 4, 16):
                tiles[t] = jnp.where(inside, 0.0, tiles[t])
                for k, one in enumerate(sets):
                    one[t] = one[t] - change[8 * t : 8 * t + 8, 128 * k : 128 * k + 128]


def factor(gram, rank, emit=None):
    row = lax.broadcasted_iota(jnp.int32, (128, 128), 0)
    col = lax.broadcasted_iota(jnp.int32, (128, 128), 1)
    keep = (row < rank) & (col < rank)
    masked = jnp.where(keep, gram, 0.0)
    eye = row == col
    trace = jnp.sum(jnp.where(eye, masked, 0.0), keepdims=True)
    delta = 0.01 * trace / jnp.full((1, 1), rank, jnp.int32).astype(F)
    shifted = masked * (1.0 / delta) + jnp.where(eye, 1.0, 0.0)
    root = jnp.broadcast_to(lax.rsqrt(delta), (16, 128))
    out = []

    def take(b, inverse, solved):
        out.append(jnp.concatenate(inverse, axis=0) * root)
        if emit is not None:
            emit(b, jnp.concatenate(solved, axis=0) * root)

    def tiles(a):
        return [a[8 * t : 8 * t + 8] for t in range(16)]

    eliminate(tiles(shifted), tiles(masked) if emit is not None else None, take)
    return jnp.where(keep, jnp.concatenate(out, axis=0), 0.0)


def dot_tn(a, b):
    return lax.dot_general(a, b, (((0,), (0,)), ((), ())), precision=HIGHEST, preferred_element_type=F)


def dot_nt(a, b):
    return lax.dot_general(a, b, (((1,), (1,)), ((), ())), precision=HIGHEST, preferred_element_type=F)


def partner_of(level, row_at, col_at):
    step = (level + 1) // 2
    odd = level % 2
    row = row_at + odd * step * (1 - 2 * ((row_at // step) % 2))
    col = col_at + (1 - odd) * step * (1 - 2 * ((col_at // step) % 2))
    return row, col


def combine(taps):
    sub = lax.broadcasted_iota(jnp.int32, (16, 256), 0)
    lane = lax.broadcasted_iota(jnp.int32, (16, 256), 1)
    count = taps.shape[2]

    def of(which, index):
        return jnp.where(sub == 0, taps[0, which, index], taps[1, which, index])

    first = jnp.zeros((16, 256), F)
    for a in range(count):
        first = jnp.where(lane == a, of(0, a), first)
    total = jnp.zeros((16, 256), F)
    for b in range(count):
        total = total + (pltpu.roll(first, 4 * b, 1) if b else first) * of(1, b)
    return total.astype(BF)


def stretched(line, length, width):
    sub = lax.broadcasted_iota(jnp.int32, (8, width), 0)
    base = jnp.broadcast_to(line, (8, width))
    for bit in (1, 2, 4):
        base = jnp.where((sub // bit) % 2 == 1, pltpu.roll(base, bit, 1), base)
    tiles = [base] + [pltpu.roll(base, 8 * t, 1) for t in range(1, length // 8)]
    return jnp.concatenate(tiles, axis=0)


def body(
    taps_far, ranks_far, probes, sketch, moved_ref,
    tall, broad, mix, across, part, gram_ref, weights_ref, own, other, taps, ranks,
    small_sem, own_sem, row_send, row_recv, col_send, col_recv, swap_send, swap_recv,
):
    n_x, n_y = lax.axis_size("tx"), lax.axis_size("ty")
    row_at, col_at = lax.axis_index("tx"), lax.axis_index("ty")
    has_up, has_down = row_at > 0, row_at < n_x - 1
    has_left, has_right = col_at > 0, col_at < n_y - 1
    up, down = (row_at - 1, col_at), (row_at + 1, col_at)
    left, right = (row_at, col_at - 1), (row_at, col_at + 1)
    sides = ((has_up, up), (has_down, down), (has_left, left), (has_right, right))

    load = pltpu.make_async_copy(probes, tall.at[pl.ds(REACH, SIDE)], own_sem)
    load.start()
    small = [
        pltpu.make_async_copy(taps_far, taps, small_sem.at[0]),
        pltpu.make_async_copy(ranks_far, ranks, small_sem.at[1]),
    ]
    for copy in small:
        copy.start()
    barrier = pltpu.get_barrier_semaphore()
    for there, device in sides:
        @pl.when(there)
        def _():
            pl.semaphore_signal(barrier, inc=1, device_id=device, device_id_type=MESH)

    @pl.loop(1, 5)
    def _(level):
        pl.semaphore_signal(
            barrier, inc=1, device_id=partner_of(level, row_at, col_at), device_id_type=MESH
        )

    peers = [there.astype(jnp.int32) for there, _ in sides]
    pl.semaphore_wait(barrier, peers[0] + peers[1] + peers[2] + peers[3] + 4)

    def is_last(step):
        return isinstance(step, int) and step >= STEPS - 1

    def size_of(step):
        return 4 if is_last(step) else 8

    def first_row(step, block):
        if is_last(step):
            return (4, 120)[block] if step == STEPS - 1 else (0, 124)[block]
        return pl.multiple_of(8 * (7 - step + block * (1 + 2 * step)), 8)

    def row_copy(to_down, step, first):
        count = 24 if first else size_of(step)
        far = 48 + 4 * step if is_last(step) else 8 * step + 24
        if to_down:
            source, target, device, way = SIDE - far, REACH - far, down, 0
        else:
            source, target, device, way = far - count, REACH + SIDE + far - count, up, 1
        return pltpu.make_async_remote_copy(
            src_ref=probes.at[pl.ds(source, count)],
            dst_ref=tall.at[pl.ds(target, count)],
            send_sem=row_send.at[way, step],
            recv_sem=row_recv.at[way, step],
            device_id=device,
            device_id_type=MESH,
        )

    def col_copy(to_right, step, low):
        rows, count = first_row(step, 0 if low else 1), size_of(step)
        if to_right:
            source, target, device, way = SIDE, 0, right, 0
        else:
            source, target, device, way = REACH, REACH + SIDE, left, 1
        half = 0 if low else 1
        return pltpu.make_async_remote_copy(
            src_ref=broad.at[pl.ds(rows, count), pl.ds(source, REACH)],
            dst_ref=broad.at[pl.ds(rows, count), pl.ds(target, REACH)],
            send_sem=col_send.at[way, half, step],
            recv_sem=col_recv.at[way, half, step],
            device_id=device,
            device_id_type=MESH,
        )

    def each(action, step, first=False):
        for there, to_down in ((has_down, True), (has_up, False)):
            @pl.when(there)
            def _():
                action(row_copy(to_down, step, first))

    def each_arrival(step, first=False):
        for there, to_down in ((has_up, True), (has_down, False)):
            @pl.when(there)
            def _():
                row_copy(to_down, step, first).wait_recv()

    start = lambda copy: copy.start()
    sent = lambda copy: copy.wait_send()
    each(start, 0, True)
    each(start, 1)
    for copy in small:
        copy.wait()
    lines = combine(taps)
    wide = mix.shape[1]
    spot = lax.broadcasted_iota(jnp.int32, (256, wide), 1)
    spread = jnp.where(spot == 16 * lax.broadcasted_iota(jnp.int32, (256, wide), 0), 1.0, 0.0)
    line_x = jnp.dot(lines, spread.astype(BF), preferred_element_type=F)[0:1]
    line_y = jnp.concatenate([lines[1:2].astype(F), jnp.zeros((1, 128), F)], axis=1)
    mix[...] = stretched(line_x, 128, wide).astype(BF)
    across[...] = stretched(line_y, 128, across.shape[1]).astype(BF)

    @pl.when(jnp.logical_not(has_up))
    def _():
        tall[pl.ds(0, REACH)] = jnp.zeros((REACH, SIDE, SIDE), BF)

    @pl.when(jnp.logical_not(has_down))
    def _():
        tall[pl.ds(REACH + SIDE, REACH)] = jnp.zeros((REACH, SIDE, SIDE), BF)

    @pl.when(jnp.logical_not(has_left))
    def _():
        broad[:, pl.ds(0, REACH)] = jnp.zeros((SIDE, REACH, SIDE), BF)

    @pl.when(jnp.logical_not(has_right))
    def _():
        broad[:, pl.ds(REACH + SIDE, REACH)] = jnp.zeros((SIDE, REACH, SIDE), BF)

    gram_ref[...] = jnp.zeros_like(gram_ref)
    load.wait()

    def place(step, block, group):
        rows = pl.multiple_of(8 * (7 - step + block * (1 + 2 * step)), 8)
        return 4 * block + group, rows, 32 * group

    def aligned(cols):
        return cols if isinstance(cols, int) else pl.multiple_of(cols, 16)

    def columns(rows, depth, cols):
        return jnp.concatenate(
            [
                tall[pl.ds(rows, depth), pl.ds(aligned(cols + 16 * k), 16)].reshape(depth * 16, SIDE)
                for k in range(2)
            ],
            axis=1,
        )

    def begin_rows(step):
        @pl.loop(0, 4)
        def _(group):
            for block in range(2):
                index, rows, cols = place(step, block, group)
                near = 8 * (1 - block)
                part[index] = jnp.dot(
                    mix[:, 16 * near : 16 * near + 32 * REACH],
                    columns(rows + near, 2 * REACH, cols),
                    preferred_element_type=F,
                )

    def finish_rows(step):
        for block, group in [(block, group) for block in range(2) for group in range(4)]:
            index, rows, cols = place(step, block, group)
            far = 2 * REACH * block
            newest = columns(rows + far, 8, cols)
            middle = (
                part[index]
                + jnp.dot(mix[:, 16 * far : 16 * far + 128], newest, preferred_element_type=F)
            ).astype(BF)
            for k in range(2):
                broad[pl.ds(rows, 8), pl.ds(REACH + cols + 16 * k, 16)] = middle[
                    :, SIDE * k : SIDE * (k + 1)
                ].reshape(8, 16, SIDE)

    def finish_last(step):
        second = step == STEPS
        for block, group in [(block, group) for block in range(2) for group in range(4)]:
            depth = 8 if second else 4
            half = 64 * (second == (block == 1))
            start_row = 0 if block == 0 else REACH + SIDE + REACH - 8
            shift = 0 if second or block == 1 else 4
            offset = 16 * (2 * REACH * block + shift)
            newest = columns(start_row + shift, depth, 32 * group)
            middle = (
                part[4 * block + group, half : half + 64]
                + jnp.dot(
                    mix[half : half + 64, offset : offset + 16 * depth],
                    newest,
                    preferred_element_type=F,
                )
            ).astype(BF)
            rows = first_row(step, block)
            for k in range(2):
                broad[pl.ds(rows, 4), pl.ds(REACH + 32 * group + 16 * k, 16)] = middle[
                    :, SIDE * k : SIDE * (k + 1)
                ].reshape(4, 16, SIDE)

    def send_cols(step):
        for there, to_right in ((has_right, True), (has_left, False)):
            for low in (True, False):
                @pl.when(there)
                def _():
                    col_copy(to_right, step, low).start()

    def filter_cols(step):
        for there, to_right in ((has_left, True), (has_right, False)):
            for low in (True, False):
                @pl.when(there)
                def _():
                    col_copy(to_right, step, low).wait_recv()

        for block in range(2):
            rows = first_row(step, block)
            for k in range(size_of(step) // 2):
                pair = [broad[rows + 2 * k + m] for m in range(2)]
                result = jnp.dot(
                    across[:, : SIDE + 2 * REACH],
                    jnp.concatenate(pair, axis=1),
                    preferred_element_type=F,
                ).astype(BF)
                for m in range(2):
                    sketch[rows + 2 * k + m] = result[:, SIDE * m : SIDE * (m + 1)]
            flat = sketch[pl.ds(rows, size_of(step))].reshape(size_of(step) * SIDE, SIDE)
            gram_ref[...] += lax.dot_general(
                flat, flat, (((0,), (0,)), ((), ())), preferred_element_type=F
            )

    each_arrival(0, True)
    begin_rows(0)

    @pl.loop(0, STEPS - 1)
    def _(step):
        @pl.when(step > 0)
        def _():
            each_arrival(step)
        finish_rows(step)
        send_cols(step)

        @pl.when(step == 0)
        def _():
            each(sent, 0, True)

        @pl.when(step > 0)
        def _():
            each(sent, step)

        @pl.when(step < STEPS - 3)
        def _():
            each(start, step + 2)

        @pl.when(step == STEPS - 3)
        def _():
            each(start, STEPS - 1)

        @pl.when(step == STEPS - 2)
        def _():
            each(start, STEPS)

        begin_rows(step + 1)

        @pl.when(step > 0)
        def _():
            filter_cols(step - 1)

    last = (STEPS - 1, STEPS)
    for step in last:
        each_arrival(step)
        finish_last(step)
        send_cols(step)
        if step == last[0]:
            filter_cols(jnp.int32(STEPS - 2))
    for step in last:
        filter_cols(step)
        each(sent, step)

    def swap(level, b):
        here = pl.ds(16 * b, 16)
        return pltpu.make_async_remote_copy(
            src_ref=own.at[level, here],
            dst_ref=other.at[level, here],
            send_sem=swap_send.at[level, b],
            recv_sem=swap_recv.at[level, b],
            device_id=partner_of(level + 1, row_at, col_at),
            device_id_type=MESH,
        )

    def rank_at(level, span_x, span_y):
        return ranks[level, col_at - col_at % span_y, row_at - row_at % span_x]

    gram_ref[...] = gram_ref[...] * (1.0 / (SIDE * SIDE))

    @pl.loop(0, 4)
    def _(level):
        span_x = jnp.where(level < 1, 1, jnp.where(level < 3, 2, 4))
        span_y = jnp.where(level < 2, 1, 2)

        def emit(b, solved):
            own[level, 16 * b : 16 * b + 16] = solved
            swap(level, b).start()

        linv = factor(gram_ref[...], rank_at(level, span_x, span_y), emit)

        @pl.when(level == 0)
        def _():
            weights_ref[...] = linv.T.astype(BF)

        @pl.when(level > 0)
        def _():
            moved_ref[0, 0, level - 1] = dot_nt(own[level - 1], linv)
        weights = weights_ref[...]
        zero = jnp.zeros_like(weights)
        twice = jnp.concatenate(
            [
                jnp.concatenate([weights, zero], axis=1),
                jnp.concatenate([zero, weights], axis=1),
            ],
            axis=0,
        )
        for group in range(4):
            rows = pl.multiple_of(32 * level + 8 * group, 8)
            pair = [sketch[pl.ds(rows + 4 * k, 4)].reshape(4 * SIDE, SIDE) for k in range(2)]
            both = jnp.dot(jnp.concatenate(pair, axis=1), twice, preferred_element_type=F)
            for k in range(2):
                sketch[pl.ds(rows + 4 * k, 4)] = (
                    both[:, SIDE * k : SIDE * (k + 1)].astype(BF).reshape(4, SIDE, SIDE)
                )
        for b in range(8):
            swap(level, b).wait_recv()
        both = jnp.concatenate([own[level], other[level]], axis=0)
        gram_ref[...] = dot_tn(both, both) * 0.5

    linv = factor(gram_ref[...], rank_at(4, 4, 4))
    moved_ref[0, 0, 3] = dot_nt(own[3], linv)

    @pl.loop(0, 4)
    def _(level):
        for b in range(8):
            swap(level, b).wait_send()

    def sent_cols(step):
        for there, to_right in ((has_right, True), (has_left, False)):
            for low in (True, False):
                @pl.when(there)
                def _():
                    col_copy(to_right, step, low).wait_send()

    @pl.loop(0, STEPS - 1)
    def _(step):
        sent_cols(step)

    for step in last:
        sent_cols(step)


def compress(taps, ranks, probes):
    depth = 8 + 2 * REACH
    return pl.pallas_call(
        body,
        out_shape=(
            jax.ShapeDtypeStruct((SIDE, SIDE, SIDE), BF),
            jax.ShapeDtypeStruct((1, 1, 4, SIDE, SIDE), F),
        ),
        in_specs=[
            pl.BlockSpec(memory_space=pltpu.HBM),
            pl.BlockSpec(memory_space=pltpu.HBM),
            pl.BlockSpec(memory_space=pltpu.HBM),
        ],
        out_specs=(pl.BlockSpec(memory_space=pltpu.VMEM),) * 2,
        scratch_shapes=[
            pltpu.VMEM((SIDE + 2 * REACH, SIDE, SIDE), BF),
            pltpu.VMEM((SIDE, SIDE + 2 * REACH, SIDE), BF),
            pltpu.VMEM((SIDE, 16 * depth), BF),
            pltpu.VMEM((SIDE, 384), BF),
            pltpu.VMEM((8, SIDE, 2 * SIDE), F),
            pltpu.VMEM((SIDE, SIDE), F),
            pltpu.VMEM((SIDE, SIDE), BF),
            pltpu.VMEM((4, SIDE, SIDE), F),
            pltpu.VMEM((4, SIDE, SIDE), F),
            pltpu.SMEM(taps.shape, F),
            pltpu.SMEM(ranks.shape, jnp.int32),
            pltpu.SemaphoreType.DMA((2,)),
            pltpu.SemaphoreType.DMA,
            pltpu.SemaphoreType.DMA((2, STEPS + 1)),
            pltpu.SemaphoreType.DMA((2, STEPS + 1)),
            pltpu.SemaphoreType.DMA((2, 2, STEPS + 1)),
            pltpu.SemaphoreType.DMA((2, 2, STEPS + 1)),
            pltpu.SemaphoreType.DMA((4, 8)),
            pltpu.SemaphoreType.DMA((4, 8)),
        ],
        compiler_params=pltpu.CompilerParams(
            collective_id=0, has_side_effects=True, vmem_limit_bytes=48 * 2**20
        ),
        name="compress",
    )(*[pltpu.with_memory_space_constraint(a, pltpu.HBM) for a in (taps, ranks)], probes)


def store_kernel(basis, moved, basis_out, moved_out, sems):
    rows = SIDE // 8
    copies = [pltpu.make_async_copy(moved, moved_out, sems.at[8])]
    for index in range(8):
        here = pl.ds(rows * index, rows)
        copies.append(pltpu.make_async_copy(basis.at[here], basis_out.at[here], sems.at[index]))
    for copy in copies:
        copy.start()
    for copy in copies:
        copy.wait()


def store(basis, moved):
    return pl.pallas_call(
        store_kernel,
        out_shape=(
            jax.ShapeDtypeStruct(basis.shape, BF),
            jax.ShapeDtypeStruct(moved.shape, F),
        ),
        in_specs=[pl.BlockSpec(memory_space=pltpu.VMEM)] * 2,
        out_specs=(pl.BlockSpec(memory_space=pltpu.HBM),) * 2,
        scratch_shapes=[pltpu.SemaphoreType.DMA((9,))],
        compiler_params=pltpu.CompilerParams(vmem_limit_bytes=16 * 2**20),
        name="store",
    )(basis, moved)


def local(probes, filter_taps, cluster_ranks):
    return store(*compress(filter_taps, jnp.swapaxes(cluster_ranks, 1, 2), probes))


def solution(mesh):
    in_specs = (P("tx", "ty", None), P(), P())
    out_specs = (P("tx", "ty", None), P("tx", "ty", None, None, None))
    return jax.shard_map(local, mesh=mesh, in_specs=in_specs, out_specs=out_specs, check_vma=False)
```

```python
import jax
import jax.numpy as jnp
from jax import lax
from jax.experimental import pallas as pl
from jax.experimental.pallas import tpu as pltpu
from jax.sharding import PartitionSpec as P

HIGHEST = lax.Precision.HIGHEST
F = jnp.float32
BF = jnp.bfloat16
REACH = 80
SIDE = 128
STEPS = 8
MESH = pl.DeviceIdType.MESH


def lane_of(x, i):
    return jnp.broadcast_to(x[:, i : i + 1], (8, 128))


def row_of(x, i):
    return jnp.broadcast_to(x[i : i + 1, :], (8, 128))


def split(a):
    one = a.astype(BF)
    rest = a - one.astype(F)
    two = rest.astype(BF)
    return one, two, (rest - two.astype(F)).astype(BF)


def eliminate(tiles, extra, emit):
    sub = lax.broadcasted_iota(jnp.int32, (8, 128), 0)
    lane = lax.broadcasted_iota(jnp.int32, (8, 128), 1)
    zero = jnp.zeros((8, 128), F)
    sets = [list(tiles)] + ([list(extra)] if extra is not None else [])
    tiles = sets[0]
    for b in range(8):
        j = 16 * b
        near = range(2 * b + 2, min(2 * b + 4, 16))
        body = [2 * b, 2 * b + 1, *near]
        cols = {
            t: [lane_of(tiles[t], j + c) if t > 2 * b or c < 8 else None for c in range(16)]
            for t in body
        }
        inside = (lane >= j) & (lane < j + 16)
        for t in body:
            h = t - 2 * b
            unit = jnp.where(lane - j == sub + 8 * h, 1.0, 0.0) if h < 2 else 0.0
            tiles[t] = jnp.where(inside, unit, tiles[t])
        kept = [[zero, zero] for _ in sets]
        raw, scaled = [zero, zero], [[zero, zero] for _ in sets]
        for c in range(16):
            h, s = divmod(c, 8)
            first = 2 * b + h
            pivot = row_of(cols[first][c], s)
            inv, root = 1.0 / pivot, lax.rsqrt(pivot)
            lines = [row_of(one[first], s) for one in sets]
            for k, line in enumerate(lines):
                kept[k][h] = jnp.where(sub == s, line * root, kept[k][h])
                if b < 6:
                    scaled[k][h] = jnp.where(sub == s, line * inv, scaled[k][h])
            if b < 6:
                raw[h] = jnp.where(sub == s, lines[0], raw[h])
            for t in body[h:]:
                ratio = cols[t][c] * inv
                for e in range(c + 1, 16):
                    if t >= 2 * b + e // 8:
                        entry = row_of(cols[2 * b + e // 8][c], e % 8)
                        cols[t][e] = cols[t][e] - ratio * entry
                for k, line in enumerate(lines):
                    sets[k][t] = sets[k][t] - ratio * line
        emit(
            b,
            [jnp.where(lane <= j + 8 * h + sub, kept[0][h], 0.0) for h in range(2)],
            kept[1] if len(sets) > 1 else None,
        )
        if b < 6:
            a1, a2, a3 = split(jnp.concatenate(raw, axis=0))
            wide = [jnp.concatenate(pair, axis=0) for pair in scaled]
            b1, b2, b3 = split(jnp.concatenate(wide, axis=1))
            change = lax.dot_general(
                jnp.concatenate([a1, a1, a2, a2, a1, a3], axis=0),
                jnp.concatenate([b1, b2, b1, b2, b3, b1], axis=0),
                (((0,), (0,)), ((), ())),
                preferred_element_type=F,
            )
            for t in range(2 * b + 4, 16):
                tiles[t] = jnp.where(inside, 0.0, tiles[t])
                for k, one in enumerate(sets):
                    one[t] = one[t] - change[8 * t : 8 * t + 8, 128 * k : 128 * k + 128]


def factor(gram, rank, emit=None):
    row = lax.broadcasted_iota(jnp.int32, (128, 128), 0)
    col = lax.broadcasted_iota(jnp.int32, (128, 128), 1)
    keep = (row < rank) & (col < rank)
    masked = jnp.where(keep, gram, 0.0)
    eye = row == col
    trace = jnp.sum(jnp.where(eye, masked, 0.0), keepdims=True)
    delta = 0.01 * trace / jnp.full((1, 1), rank, jnp.int32).astype(F)
    shifted = masked * (1.0 / delta) + jnp.where(eye, 1.0, 0.0)
    root = jnp.broadcast_to(lax.rsqrt(delta), (16, 128))
    out = []

    def take(b, inverse, solved):
        out.append(jnp.concatenate(inverse, axis=0) * root)
        if emit is not None:
            emit(b, jnp.concatenate(solved, axis=0) * root)

    def tiles(a):
        return [a[8 * t : 8 * t + 8] for t in range(16)]

    eliminate(tiles(shifted), tiles(masked) if emit is not None else None, take)
    return jnp.where(keep, jnp.concatenate(out, axis=0), 0.0)


def dot_tn(a, b):
    return lax.dot_general(a, b, (((0,), (0,)), ((), ())), precision=HIGHEST, preferred_element_type=F)


def dot_nt(a, b):
    return lax.dot_general(a, b, (((1,), (1,)), ((), ())), precision=HIGHEST, preferred_element_type=F)


def partner_of(level, row_at, col_at):
    step = (level + 1) // 2
    odd = level % 2
    row = row_at + odd * step * (1 - 2 * ((row_at // step) % 2))
    col = col_at + (1 - odd) * step * (1 - 2 * ((col_at // step) % 2))
    return row, col


def combine(taps):
    sub = lax.broadcasted_iota(jnp.int32, (16, 256), 0)
    lane = lax.broadcasted_iota(jnp.int32, (16, 256), 1)
    count = taps.shape[2]

    def of(which, index):
        return jnp.where(sub == 0, taps[0, which, index], taps[1, which, index])

    first = jnp.zeros((16, 256), F)
    for a in range(count):
        first = jnp.where(lane == a, of(0, a), first)
    total = jnp.zeros((16, 256), F)
    for b in range(count):
        total = total + (pltpu.roll(first, 4 * b, 1) if b else first) * of(1, b)
    return total.astype(BF)


def stretched(line, length, width):
    sub = lax.broadcasted_iota(jnp.int32, (8, width), 0)
    base = jnp.broadcast_to(line, (8, width))
    for bit in (1, 2, 4):
        base = jnp.where((sub // bit) % 2 == 1, pltpu.roll(base, bit, 1), base)
    tiles = [base] + [pltpu.roll(base, 8 * t, 1) for t in range(1, length // 8)]
    return jnp.concatenate(tiles, axis=0)


def body(
    taps_far, ranks_far, probes, sketch, moved_ref,
    tall, broad, mix, across, part, gram_ref, weights_ref, own, other, taps, ranks,
    small_sem, own_sem, row_send, row_recv, col_send, col_recv, swap_send, swap_recv,
):
    n_x, n_y = lax.axis_size("tx"), lax.axis_size("ty")
    row_at, col_at = lax.axis_index("tx"), lax.axis_index("ty")
    has_up, has_down = row_at > 0, row_at < n_x - 1
    has_left, has_right = col_at > 0, col_at < n_y - 1
    up, down = (row_at - 1, col_at), (row_at + 1, col_at)
    left, right = (row_at, col_at - 1), (row_at, col_at + 1)
    sides = ((has_up, up), (has_down, down), (has_left, left), (has_right, right))

    load = pltpu.make_async_copy(probes, tall.at[pl.ds(REACH, SIDE)], own_sem)
    load.start()
    small = [
        pltpu.make_async_copy(taps_far, taps, small_sem.at[0]),
        pltpu.make_async_copy(ranks_far, ranks, small_sem.at[1]),
    ]
    for copy in small:
        copy.start()
    barrier = pltpu.get_barrier_semaphore()
    for there, device in sides:
        @pl.when(there)
        def _():
            pl.semaphore_signal(barrier, inc=1, device_id=device, device_id_type=MESH)

    @pl.loop(1, 5)
    def _(level):
        pl.semaphore_signal(
            barrier, inc=1, device_id=partner_of(level, row_at, col_at), device_id_type=MESH
        )

    peers = [there.astype(jnp.int32) for there, _ in sides]
    pl.semaphore_wait(barrier, peers[0] + peers[1] + peers[2] + peers[3] + 4)

    def is_last(step):
        return isinstance(step, int) and step >= STEPS - 1

    def size_of(step):
        return 4 if is_last(step) else 8

    def first_row(step, block):
        if is_last(step):
            return (4, 120)[block] if step == STEPS - 1 else (0, 124)[block]
        return pl.multiple_of(8 * (7 - step + block * (1 + 2 * step)), 8)

    def row_copy(to_down, step, first):
        count = 24 if first else size_of(step)
        far = 48 + 4 * step if is_last(step) else 8 * step + 24
        if to_down:
            source, target, device, way = SIDE - far, REACH - far, down, 0
        else:
            source, target, device, way = far - count, REACH + SIDE + far - count, up, 1
        return pltpu.make_async_remote_copy(
            src_ref=probes.at[pl.ds(source, count)],
            dst_ref=tall.at[pl.ds(target, count)],
            send_sem=row_send.at[way, step],
            recv_sem=row_recv.at[way, step],
            device_id=device,
            device_id_type=MESH,
        )

    def col_copy(to_right, step, low):
        rows, count = first_row(step, 0 if low else 1), size_of(step)
        if to_right:
            source, target, device, way = SIDE, 0, right, 0
        else:
            source, target, device, way = REACH, REACH + SIDE, left, 1
        half = 0 if low else 1
        return pltpu.make_async_remote_copy(
            src_ref=broad.at[pl.ds(rows, count), pl.ds(source, REACH)],
            dst_ref=broad.at[pl.ds(rows, count), pl.ds(target, REACH)],
            send_sem=col_send.at[way, half, step],
            recv_sem=col_recv.at[way, half, step],
            device_id=device,
            device_id_type=MESH,
        )

    def each(action, step, first=False):
        for there, to_down in ((has_down, True), (has_up, False)):
            @pl.when(there)
            def _():
                action(row_copy(to_down, step, first))

    def each_arrival(step, first=False):
        for there, to_down in ((has_up, True), (has_down, False)):
            @pl.when(there)
            def _():
                row_copy(to_down, step, first).wait_recv()

    start = lambda copy: copy.start()
    sent = lambda copy: copy.wait_send()
    each(start, 0, True)
    each(start, 1)
    for copy in small:
        copy.wait()
    lines = combine(taps)
    wide = mix.shape[1]
    spot = lax.broadcasted_iota(jnp.int32, (256, wide), 1)
    spread = jnp.where(spot == 16 * lax.broadcasted_iota(jnp.int32, (256, wide), 0), 1.0, 0.0)
    line_x = jnp.dot(lines, spread.astype(BF), preferred_element_type=F)[0:1]
    line_y = jnp.concatenate([lines[1:2].astype(F), jnp.zeros((1, 128), F)], axis=1)
    mix[...] = stretched(line_x, 128, wide).astype(BF)
    across[...] = stretched(line_y, 128, across.shape[1]).astype(BF)

    @pl.when(jnp.logical_not(has_up))
    def _():
        tall[pl.ds(0, REACH)] = jnp.zeros((REACH, SIDE, SIDE), BF)

    @pl.when(jnp.logical_not(has_down))
    def _():
        tall[pl.ds(REACH + SIDE, REACH)] = jnp.zeros((REACH, SIDE, SIDE), BF)

    @pl.when(jnp.logical_not(has_left))
    def _():
        broad[:, pl.ds(0, REACH)] = jnp.zeros((SIDE, REACH, SIDE), BF)

    @pl.when(jnp.logical_not(has_right))
    def _():
        broad[:, pl.ds(REACH + SIDE, REACH)] = jnp.zeros((SIDE, REACH, SIDE), BF)

    gram_ref[...] = jnp.zeros_like(gram_ref)
    load.wait()

    def place(step, block, group):
        rows = pl.multiple_of(8 * (7 - step + block * (1 + 2 * step)), 8)
        return 4 * block + group, rows, 32 * group

    def aligned(cols):
        return cols if isinstance(cols, int) else pl.multiple_of(cols, 16)

    def columns(rows, depth, cols):
        return jnp.concatenate(
            [
                tall[pl.ds(rows, depth), pl.ds(aligned(cols + 16 * k), 16)].reshape(depth * 16, SIDE)
                for k in range(2)
            ],
            axis=1,
        )

    def begin_rows(step):
        @pl.loop(0, 4)
        def _(group):
            for block in range(2):
                index, rows, cols = place(step, block, group)
                near = 8 * (1 - block)
                part[index] = jnp.dot(
                    mix[:, 16 * near : 16 * near + 32 * REACH],
                    columns(rows + near, 2 * REACH, cols),
                    preferred_element_type=F,
                )

    def finish_rows(step):
        for block, group in [(block, group) for block in range(2) for group in range(4)]:
            index, rows, cols = place(step, block, group)
            far = 2 * REACH * block
            newest = columns(rows + far, 8, cols)
            middle = (
                part[index]
                + jnp.dot(mix[:, 16 * far : 16 * far + 128], newest, preferred_element_type=F)
            ).astype(BF)
            for k in range(2):
                broad[pl.ds(rows, 8), pl.ds(REACH + cols + 16 * k, 16)] = middle[
                    :, SIDE * k : SIDE * (k + 1)
                ].reshape(8, 16, SIDE)

    def finish_last(step):
        second = step == STEPS
        for block, group in [(block, group) for block in range(2) for group in range(4)]:
            depth = 8 if second else 4
            half = 64 * (second == (block == 1))
            start_row = 0 if block == 0 else REACH + SIDE + REACH - 8
            shift = 0 if second or block == 1 else 4
            offset = 16 * (2 * REACH * block + shift)
            newest = columns(start_row + shift, depth, 32 * group)
            middle = (
                part[4 * block + group, half : half + 64]
                + jnp.dot(
                    mix[half : half + 64, offset : offset + 16 * depth],
                    newest,
                    preferred_element_type=F,
                )
            ).astype(BF)
            rows = first_row(step, block)
            for k in range(2):
                broad[pl.ds(rows, 4), pl.ds(REACH + 32 * group + 16 * k, 16)] = middle[
                    :, SIDE * k : SIDE * (k + 1)
                ].reshape(4, 16, SIDE)

    def send_cols(step):
        for there, to_right in ((has_right, True), (has_left, False)):
            for low in (True, False):
                @pl.when(there)
                def _():
                    col_copy(to_right, step, low).start()

    def filter_cols(step):
        for there, to_right in ((has_left, True), (has_right, False)):
            for low in (True, False):
                @pl.when(there)
                def _():
                    col_copy(to_right, step, low).wait_recv()

        for block in range(2):
            rows = first_row(step, block)
            for k in range(size_of(step) // 2):
                pair = [broad[rows + 2 * k + m] for m in range(2)]
                result = jnp.dot(
                    across[:, : SIDE + 2 * REACH],
                    jnp.concatenate(pair, axis=1),
                    preferred_element_type=F,
                ).astype(BF)
                for m in range(2):
                    sketch[rows + 2 * k + m] = result[:, SIDE * m : SIDE * (m + 1)]
            flat = sketch[pl.ds(rows, size_of(step))].reshape(size_of(step) * SIDE, SIDE)
            gram_ref[...] += lax.dot_general(
                flat, flat, (((0,), (0,)), ((), ())), preferred_element_type=F
            )

    each_arrival(0, True)
    begin_rows(0)

    @pl.loop(0, STEPS - 1)
    def _(step):
        @pl.when(step > 0)
        def _():
            each_arrival(step)
        finish_rows(step)
        send_cols(step)

        @pl.when(step == 0)
        def _():
            each(sent, 0, True)

        @pl.when(step > 0)
        def _():
            each(sent, step)

        @pl.when(step < STEPS - 3)
        def _():
            each(start, step + 2)

        @pl.when(step == STEPS - 3)
        def _():
            each(start, STEPS - 1)

        @pl.when(step == STEPS - 2)
        def _():
            each(start, STEPS)

        begin_rows(step + 1)

        @pl.when(step > 0)
        def _():
            filter_cols(step - 1)

    last = (STEPS - 1, STEPS)
    for step in last:
        each_arrival(step)
        finish_last(step)
        send_cols(step)
        if step == last[0]:
            filter_cols(jnp.int32(STEPS - 2))
    for step in last:
        filter_cols(step)
        each(sent, step)

    pieces = ((0, 48), (48, 48), (96, 16), (112, 16))

    def swap(level, b):
        here = pl.ds(*pieces[b])
        return pltpu.make_async_remote_copy(
            src_ref=own.at[level, here],
            dst_ref=other.at[level, here],
            send_sem=swap_send.at[level, b],
            recv_sem=swap_recv.at[level, b],
            device_id=partner_of(level + 1, row_at, col_at),
            device_id_type=MESH,
        )

    def rank_at(level, span_x, span_y):
        return ranks[level, col_at - col_at % span_y, row_at - row_at % span_x]

    gram_ref[...] = gram_ref[...] * (1.0 / (SIDE * SIDE))

    @pl.loop(0, 4)
    def _(level):
        span_x = jnp.where(level < 1, 1, jnp.where(level < 3, 2, 4))
        span_y = jnp.where(level < 2, 1, 2)

        def emit(b, solved):
            own[level, 16 * b : 16 * b + 16] = solved
            for index, (first, count) in enumerate(pieces):
                if 16 * b + 16 == first + count:
                    swap(level, index).start()

        linv = factor(gram_ref[...], rank_at(level, span_x, span_y), emit)

        @pl.when(level == 0)
        def _():
            weights_ref[...] = linv.T.astype(BF)

        @pl.when(level > 0)
        def _():
            moved_ref[0, 0, level - 1] = dot_nt(own[level - 1], linv)
        weights = weights_ref[...]
        zero = jnp.zeros_like(weights)
        twice = jnp.concatenate(
            [
                jnp.concatenate([weights, zero], axis=1),
                jnp.concatenate([zero, weights], axis=1),
            ],
            axis=0,
        )
        for group in range(4):
            rows = pl.multiple_of(32 * level + 8 * group, 8)
            pair = [sketch[pl.ds(rows + 4 * k, 4)].reshape(4 * SIDE, SIDE) for k in range(2)]
            both = jnp.dot(jnp.concatenate(pair, axis=1), twice, preferred_element_type=F)
            for k in range(2):
                sketch[pl.ds(rows + 4 * k, 4)] = (
                    both[:, SIDE * k : SIDE * (k + 1)].astype(BF).reshape(4, SIDE, SIDE)
                )
        for b in range(3):
            swap(level, b).wait_recv()
        most = jnp.concatenate([own[level], other[level, 0:112]], axis=0)
        gram_ref[...] = dot_tn(most, most)
        swap(level, 3).wait_recv()
        rest = other[level, 112:128]
        gram_ref[...] = (gram_ref[...] + dot_tn(rest, rest)) * 0.5

    linv = factor(gram_ref[...], rank_at(4, 4, 4))
    moved_ref[0, 0, 3] = dot_nt(own[3], linv)

    @pl.loop(0, 4)
    def _(level):
        for b in range(4):
            swap(level, b).wait_send()

    def sent_cols(step):
        for there, to_right in ((has_right, True), (has_left, False)):
            for low in (True, False):
                @pl.when(there)
                def _():
                    col_copy(to_right, step, low).wait_send()

    @pl.loop(0, STEPS - 1)
    def _(step):
        sent_cols(step)

    for step in last:
        sent_cols(step)


def compress(taps, ranks, probes):
    depth = 8 + 2 * REACH
    return pl.pallas_call(
        body,
        out_shape=(
            jax.ShapeDtypeStruct((SIDE, SIDE, SIDE), BF),
            jax.ShapeDtypeStruct((1, 1, 4, SIDE, SIDE), F),
        ),
        in_specs=[
            pl.BlockSpec(memory_space=pltpu.HBM),
            pl.BlockSpec(memory_space=pltpu.HBM),
            pl.BlockSpec(memory_space=pltpu.HBM),
        ],
        out_specs=(pl.BlockSpec(memory_space=pltpu.VMEM),) * 2,
        scratch_shapes=[
            pltpu.VMEM((SIDE + 2 * REACH, SIDE, SIDE), BF),
            pltpu.VMEM((SIDE, SIDE + 2 * REACH, SIDE), BF),
            pltpu.VMEM((SIDE, 16 * depth), BF),
            pltpu.VMEM((SIDE, 384), BF),
            pltpu.VMEM((8, SIDE, 2 * SIDE), F),
            pltpu.VMEM((SIDE, SIDE), F),
            pltpu.VMEM((SIDE, SIDE), BF),
            pltpu.VMEM((4, SIDE, SIDE), F),
            pltpu.VMEM((4, SIDE, SIDE), F),
            pltpu.SMEM(taps.shape, F),
            pltpu.SMEM(ranks.shape, jnp.int32),
            pltpu.SemaphoreType.DMA((2,)),
            pltpu.SemaphoreType.DMA,
            pltpu.SemaphoreType.DMA((2, STEPS + 1)),
            pltpu.SemaphoreType.DMA((2, STEPS + 1)),
            pltpu.SemaphoreType.DMA((2, 2, STEPS + 1)),
            pltpu.SemaphoreType.DMA((2, 2, STEPS + 1)),
            pltpu.SemaphoreType.DMA((4, 4)),
            pltpu.SemaphoreType.DMA((4, 4)),
        ],
        compiler_params=pltpu.CompilerParams(
            collective_id=0, has_side_effects=True, vmem_limit_bytes=48 * 2**20
        ),
        name="compress",
    )(*[pltpu.with_memory_space_constraint(a, pltpu.HBM) for a in (taps, ranks)], probes)


def store_kernel(basis, moved, basis_out, moved_out, sems):
    rows = SIDE // 8
    copies = [pltpu.make_async_copy(moved, moved_out, sems.at[8])]
    for index in range(8):
        here = pl.ds(rows * index, rows)
        copies.append(pltpu.make_async_copy(basis.at[here], basis_out.at[here], sems.at[index]))
    for copy in copies:
        copy.start()
    for copy in copies:
        copy.wait()


def store(basis, moved):
    return pl.pallas_call(
        store_kernel,
        out_shape=(
            jax.ShapeDtypeStruct(basis.shape, BF),
            jax.ShapeDtypeStruct(moved.shape, F),
        ),
        in_specs=[pl.BlockSpec(memory_space=pltpu.VMEM)] * 2,
        out_specs=(pl.BlockSpec(memory_space=pltpu.HBM),) * 2,
        scratch_shapes=[pltpu.SemaphoreType.DMA((9,))],
        compiler_params=pltpu.CompilerParams(vmem_limit_bytes=16 * 2**20),
        name="store",
    )(basis, moved)


def local(probes, filter_taps, cluster_ranks):
    return store(*compress(filter_taps, jnp.swapaxes(cluster_ranks, 1, 2), probes))


def solution(mesh):
    in_specs = (P("tx", "ty", None), P(), P())
    out_specs = (P("tx", "ty", None), P("tx", "ty", None, None, None))
    return jax.shard_map(local, mesh=mesh, in_specs=in_specs, out_specs=out_specs, check_vma=False)
```
